128 devices in a mesh: rep: 4 (over z_lo, core), shard: 32 (over z_hi, x, y).
Axes of the slice: x: 4, y: 4, z: 4 (z_hi: 2, z_lo: 2; z = z_hi * 2 + z_lo), core: 2. Of those that a mesh axis runs over, the one named last changes fastest.
Arguments:
- local_layers: float32 [4, 4, 768, 768], P('rep', None, 'shard'), may hold values from -6 to 6
- global_layers: float32 [4, 768, 768], P(None, 'shard'), may hold values from -6 to 6
- momentum_layers: float32 [4, 768, 768], P(None, 'shard'), may hold values from -3 to 3
- local_embed: float32 [4, 32128, 768], P('rep', 'shard'), may hold values from -6 to 6
- global_embed: float32 [32128, 768], P('shard'), may hold values from -6 to 6
- momentum_embed: float32 [32128, 768], P('shard'), may hold values from -3 to 3
- proj_basis: float32 [768, 64], replicated, may hold values from -0.21875 to 0.21875
Outputs:
- mean_layers: float32 [4, 768, 768], P(None, 'shard')
- moment_layers: float32 [4, 768, 768], P(None, 'shard')
- weights_layers: float32 [4, 768, 768], P(None, 'shard')
- copy_layers: bfloat16 [4, 768, 768], replicated
- mean_embed: float32 [32128, 768], P('shard')
- moment_embed: float32 [32128, 768], P('shard')
- weights_embed: float32 [32128, 768], P('shard')
The draws below stay inside these ranges and needn't reach their ends.
All inputs are finite; a program needn't handle non-finite values.
Results may differ from the reference program's by a relative error of at most 0.0085.
Values may be sent and summed in bfloat16 or wider, within the bound.
A program may use at most 128 MiB of HBM per device.

```python
import jax
import jax.numpy as jnp
from jax import lax

D = 768
RANK = 64
PROJS = 4
LAYERS = 1
GROUPS = 4
VOCAB = 32128


def block_levels(stream_key, shape, cuts, low, high):
    gain, own = 1.0, jax.random.fold_in(stream_key, 6)
    for dim, parts in cuts:
        steps = jnp.exp(jax.random.uniform(jax.random.fold_in(own, dim), (parts,), jnp.float32, low / len(cuts), high / len(cuts)))
        gain = gain * jnp.repeat(steps, shape[dim] // parts).reshape([-1 if axis == dim else 1 for axis in range(len(shape))])
    return gain


def normal_values(stream_key, shape, scale, bound, cuts=(), held_as=jnp.bfloat16):
    values = scale * jax.random.normal(stream_key, shape, jnp.float32)
    if cuts:
        values = values * block_levels(stream_key, shape, cuts, -0.22, 0.18)
    return jnp.clip(values, -bound, bound).astype(held_as)


def setup_inputs(seed: int = 0) -> dict:
    streams_of = jax.random.split(jax.random.key(seed), 8)
    return {
        "local_layers": normal_values(streams_of[0], (GROUPS, LAYERS * PROJS, D, D), 1.0, 6.0, ((0, 4), (2, 32)), jnp.float32),
        "global_layers": normal_values(streams_of[1], (LAYERS * PROJS, D, D), 1.0, 6.0, ((1, 32),), jnp.float32),
        "momentum_layers": normal_values(streams_of[2], (LAYERS * PROJS, D, D), 0.5, 3.0, ((1, 32),), jnp.float32),
        "local_embed": normal_values(streams_of[3], (GROUPS, VOCAB, D), 1.0, 6.0, ((0, 4), (1, 32)), jnp.float32),
        "global_embed": normal_values(streams_of[4], (VOCAB, D), 1.0, 6.0, ((0, 32),), jnp.float32),
        "momentum_embed": normal_values(streams_of[5], (VOCAB, D), 0.5, 3.0, ((0, 32),), jnp.float32),
        "proj_basis": normal_values(streams_of[6], (D, RANK), D ** -0.5, 0.21875, (), jnp.float32),
    }


OUTER_MOMENTUM = 0.9
OUTER_RATE = 0.7


def reference(local_layers, global_layers, momentum_layers, local_embed, global_embed, momentum_embed, proj_basis):
    layer_total = jnp.zeros(global_layers.shape, jnp.float32)
    for member in range(GROUPS):
        layer_total = layer_total + (global_layers - local_layers[member])
    mean_layers = layer_total / GROUPS
    moment_layers = OUTER_MOMENTUM * momentum_layers + mean_layers
    weights_layers = global_layers - OUTER_RATE * (mean_layers + OUTER_MOMENTUM * moment_layers)
    copy_layers = weights_layers.astype(jnp.bfloat16)
    low_total = jnp.zeros((global_embed.shape[0], proj_basis.shape[1]), jnp.float32)
    for member in range(GROUPS):
        low_total = low_total + jnp.dot(global_embed - local_embed[member], proj_basis, precision=lax.Precision.HIGHEST)
    low_mean = low_total / GROUPS
    mean_embed = jnp.dot(low_mean, proj_basis.T, precision=lax.Precision.HIGHEST)
    moment_embed = OUTER_MOMENTUM * momentum_embed + mean_embed
    weights_embed = global_embed - OUTER_RATE * (mean_embed + OUTER_MOMENTUM * moment_embed)
    return (mean_layers, moment_layers, weights_layers, copy_layers, mean_embed, moment_embed, weights_embed)
```

```python
import functools

import jax
import jax.numpy as jnp
from jax import lax
from jax.experimental import pallas as pl
from jax.experimental.pallas import tpu as pltpu
from jax.sharding import PartitionSpec as P

OUTER_MOMENTUM = 0.9
OUTER_RATE = 0.7
MESH = pl.DeviceIdType.MESH
HBM = pl.BlockSpec(memory_space=pl.ANY)
VMEM = pl.BlockSpec(memory_space=pltpu.VMEM)
X, Y, Z = 0, 1, 2
ORDERS = ((X, Y, Z), (Y, Z, X), (Z, X, Y))
DELTAS = (1, 3, 2)
HALF = 512


def outer_update(mean_diff, momentum, weights):
    new_moment = OUTER_MOMENTUM * momentum + mean_diff
    new_weights = weights - OUTER_RATE * (mean_diff + OUTER_MOMENTUM * new_moment)
    return (new_moment, new_weights)


def where_am_i():
    rep, shard = lax.axis_index("rep"), lax.axis_index("shard")
    z_low, core = lax.div(rep, 2), lax.rem(rep, 2)
    z_high, x, y = lax.div(shard, 16), lax.rem(lax.div(shard, 4), 4), lax.rem(shard, 4)
    return [x, y, z_high * 2 + z_low], core


def device(at, core):
    x, y, z = at
    return (lax.rem(z, 2) * 2 + core, lax.div(z, 2) * 16 + x * 4 + y)


def moved(at, axis, step):
    return [lax.rem(c + step, 4) if i == axis else c for i, c in enumerate(at)]


def piece(gathered, at, core, part):
    x, y, z = (slice(None) if c is None else c for c in at)
    z_low, z_high = (z, z) if isinstance(z, slice) else (lax.rem(z, 2), lax.div(z, 2))
    return gathered.at[z_low, core, z_high, x, y, part]


def exchange_kernel(
    ll, gl, ml, le, ge, me, bt,
    gathered, ge_v, me_v, low_total, layer_total,
    ll_v, gl_v, ml_v, ll_other, part_sum, part_other, le_v, bt_v, low, low_in, low_half, low_other,
    load_sem, rep_send, rep_recv, ring_send, ring_recv, pair_send, pair_recv,
):
    at, core = where_am_i()
    other = 1 - core
    z_low = lax.rem(at[Z], 2)
    twin_at = [at[X], at[Y], at[Z] + 1 - 2 * z_low]
    pair, twin = device(at, other), device(twin_at, core)
    rows = le.shape[0]

    def remote(src, dst, sems, i, to):
        send, recv = sems
        return pltpu.make_async_remote_copy(src, dst, send.at[i], recv.at[i], device_id=to, device_id_type=MESH)

    loads = [
        pltpu.make_async_copy(ll.at[:, core], ll_v, load_sem.at[0]),
        pltpu.make_async_copy(gl.at[:, core], gl_v, load_sem.at[1]),
        pltpu.make_async_copy(ml.at[z_low, core], ml_v, load_sem.at[2]),
        pltpu.make_async_copy(bt, bt_v, load_sem.at[3]),
        pltpu.make_async_copy(le, le_v, load_sem.at[4]),
        pltpu.make_async_copy(ge, ge_v, load_sem.at[5]),
        pltpu.make_async_copy(me, me_v, load_sem.at[6]),
    ]
    for load in loads:
        load.start()

    barrier = pltpu.get_barrier_semaphore()
    peers = [pair] + [device(moved(at, axis, step), core) for axis in (X, Y, Z) for step in DELTAS]
    for peer in peers:
        pl.semaphore_signal(barrier, inc=1, device_id=peer, device_id_type=MESH)
    pl.semaphore_wait(barrier, len(peers))

    rep = (rep_send, rep_recv)
    to_pair = remote(ll.at[:, other], ll_other, rep, 0, pair)
    to_pair.start()
    loads[0].wait()
    loads[1].wait()
    to_pair.wait_recv()
    part_sum[...] = (gl_v[...] - ll_v[...]) + (gl_v[...] - ll_other[...])
    first = remote(part_sum.at[1 - z_low], part_other.at[1 - z_low], rep, 1, twin)
    second = remote(part_sum.at[z_low], part_other.at[z_low], rep, 2, twin)
    first.start()
    second.start()

    loads[3].wait()
    loads[4].wait()
    loads[5].wait()
    basis = bt_v[...].astype(jnp.bfloat16)
    none = jnp.zeros_like(basis)
    left, right = jnp.concatenate([basis, none], 0), jnp.concatenate([none, basis], 0)
    nt = (((1,), (1,)), ((), ()))
    for start in range(0, HALF, 128):
        tail = min(128, rows - HALF - start)
        a, b = pl.ds(start, 128), pl.ds(HALF + start, tail)
        da = (ge_v[a, :] - le_v[a, :]).astype(jnp.bfloat16)
        db = (ge_v[b, :] - le_v[b, :]).astype(jnp.bfloat16)
        pa = lax.dot_general(da, left, nt, preferred_element_type=jnp.float32)
        pb = lax.dot_general(db, right, nt, preferred_element_type=jnp.float32)
        low[a, :] = pa
        low[pl.ds(start, tail), :] = low[pl.ds(start, tail), :] + pb
    quarter = HALF // 2
    mine, theirs = pl.ds(core * quarter, quarter), pl.ds(other * quarter, quarter)
    low_to_pair = remote(low.at[theirs], low_in, rep, 3, pair)
    low_to_pair.start()

    loads[2].wait()
    first_in = remote(part_sum.at[z_low], part_other.at[z_low], rep, 1, twin)
    first_in.wait_recv()
    mean = (part_sum[z_low] + part_other[z_low]) / 4
    _, weights = outer_update(mean, ml_v[...], gl_v[z_low])
    gathered[z_low, core, lax.div(at[Z], 2), at[X], at[Y]] = weights.astype(jnp.bfloat16).reshape(3, 8, 768)

    ring, pairs = (ring_send, ring_recv), (pair_send, pair_recv)
    started, expected = [], []

    def send(where, part, slot, to):
        copy = remote(piece(gathered, where, core, part), piece(gathered, where, core, part), ring, part * 18 + slot, to)
        copy.start()
        started.append(copy)

    def arrive(where, part, slot):
        ref = piece(gathered, where, core, part)
        remote(ref, ref, ring, part * 18 + slot, pair).wait_recv()
        share(where, part, slot)

    def share(where, part, slot):
        ref = piece(gathered, where, core, part)
        copy = remote(ref, ref, pairs, part * 19 + slot, pair)
        copy.start()
        started.append(copy)
        back = piece(gathered, where, other, part)
        expected.append(remote(back, back, pairs, part * 19 + slot, pair))

    def opened(where, *axes):
        return [None if i in axes else c for i, c in enumerate(where)]

    for part, (d1, d2, d3) in enumerate(ORDERS):
        for i, step in enumerate(DELTAS):
            send(at, part, i, device(moved(at, d1, step), core))
    for part in range(3):
        share(at, part, 18)

    low_to_pair.wait_recv()
    half = low[mine, :] + low_in[...]
    low_half[...] = half.astype(jnp.bfloat16)
    low_to_twin = remote(low_half, low_other, rep, 4, twin)
    low_to_twin.start()

    for part, (d1, d2, d3) in enumerate(ORDERS):
        for i, step in enumerate(DELTAS):
            arrive(moved(at, d1, 4 - step), part, i)
        row = opened(at, d1)
        for i, step in enumerate(DELTAS):
            send(row, part, 3 + i, device(moved(at, d2, step), core))
        for i, step in enumerate((1, 3)):
            send(row, part, 6 + i, device(moved(at, d3, step), core))

    low_to_twin.wait_recv()
    low_total[mine, :] = low_half[...].astype(jnp.float32) + low_other[...].astype(jnp.float32)
    low_back = remote(low_total.at[mine], low_total.at[mine], rep, 5, pair)
    low_back.start()

    second_in = remote(part_sum.at[1 - z_low], part_other.at[1 - z_low], rep, 2, twin)
    second_in.wait_recv()
    layer_total[:, core] = part_sum[...] + part_other[...]
    total_back = remote(layer_total.at[:, core], layer_total.at[:, core], rep, 6, pair)
    total_back.start()

    for j, back in enumerate(DELTAS):
        for part, (d1, d2, d3) in enumerate(ORDERS):
            row = opened(moved(at, d2, 4 - back), d1)
            arrive(row, part, 3 + j)
            for i, step in enumerate((1, 3)):
                send(row, part, 8 + 2 * j + i, device(moved(at, d3, step), core))

    for j, back in enumerate((0,) + DELTAS):
        for part, (d1, d2, d3) in enumerate(ORDERS):
            for i, step in enumerate((1, 3)):
                row = opened(moved(moved(at, d2, 4 - back), d3, 4 - step), d1)
                arrive(row, part, 6 + 2 * j + i)
                if j // 2 == i:
                    send(row, part, 14 + j, device(moved(at, d3, step), core))
    for j, back in enumerate((0,) + DELTAS):
        for part, (d1, d2, d3) in enumerate(ORDERS):
            arrive(opened(moved(moved(at, d2, 4 - back), d3, 2), d1), part, 14 + j)

    remote(low_total.at[theirs], low_total.at[theirs], rep, 5, pair).wait_recv()
    remote(layer_total.at[:, other], layer_total.at[:, other], rep, 6, pair).wait_recv()
    for copy in expected:
        copy.wait_recv()
    for copy in started + [to_pair, first, second, low_to_pair, low_to_twin, low_back, total_back]:
        copy.wait_send()
    loads[6].wait()


def finish_kernel(
    gathered, ge_v, me_v, low_total, layer_total, bt_v, gl_v, ml_v,
    mean_l, moment_l, weights_l, copy_l, mean_e, moment_e, weights_e,
    mean_lv, moment_lv, weights_lv, mean_v, moment_v, weights_v, sem, sem_e,
):
    rows = ge_v.shape[0]
    copies = []

    def put(src, dst, s):
        copy = pltpu.make_async_copy(src, dst, s)
        copy.start()
        copies.append(copy)

    put(gathered, copy_l, sem.at[0])
    basis = bt_v[...]
    high = basis.astype(jnp.bfloat16)
    none = jnp.zeros_like(high)
    left = jnp.concatenate([high, none, high, none], 0)
    right = jnp.concatenate([none, high, none, high], 0)
    for n, start in enumerate(range(0, rows, 128)):
        size = min(128, rows - start)
        packed = low_total[pl.ds(start % HALF, size), :] / 4
        top = packed.astype(jnp.bfloat16)
        rest = (packed - top.astype(jnp.float32)).astype(jnp.bfloat16)
        at = pl.ds(start, size)
        mean = jnp.dot(
            jnp.concatenate([top, rest], 1), left if start < HALF else right, preferred_element_type=jnp.float32
        )
        moment, weights = outer_update(mean, me_v[at, :], ge_v[at, :])
        for k, (value, buf, out) in enumerate(
            ((mean, mean_v, mean_e), (moment, moment_v, moment_e), (weights, weights_v, weights_e))
        ):
            buf[at, :] = value
            put(buf.at[at], out.at[at], sem_e.at[3 * n + k])
    mean = layer_total[...] / 4
    moment, weights = outer_update(mean, ml_v[...], gl_v[...])
    for k, (value, buf, out) in enumerate(
        ((mean, mean_lv, mean_l), (moment, moment_lv, moment_l), (weights, weights_lv, weights_l))
    ):
        buf[...] = value
        put(buf, out, sem.at[1 + k])
    for copy in copies:
        copy.wait()


def body(local_layers, global_layers, momentum_layers, local_embed, global_embed, momentum_embed, proj_basis):
    rows = global_embed.shape[0]
    grouped = (2, 2, 24, 768)
    ll, gl, ml = (a.reshape(grouped) for a in (local_layers, global_layers, momentum_layers))
    bt = proj_basis.T
    f32, bf16 = jnp.float32, jnp.bfloat16
    dma = pltpu.SemaphoreType.DMA
    gathered, ge_v, me_v, low_total, layer_total = pl.pallas_call(
        exchange_kernel,
        out_shape=(
            pltpu.VMEM((2, 2, 2, 4, 4, 3, 8, 768), bf16),
            pltpu.VMEM((rows, 768), f32),
            pltpu.VMEM((rows, 768), f32),
            pltpu.VMEM((HALF, 128), f32),
            pltpu.VMEM(grouped, f32),
        ),
        in_specs=[HBM] * 7,
        out_specs=(VMEM,) * 5,
        scratch_shapes=[
            pltpu.VMEM((2, 24, 768), f32),
            pltpu.VMEM((2, 24, 768), f32),
            pltpu.VMEM((24, 768), f32),
            pltpu.VMEM((2, 24, 768), f32),
            pltpu.VMEM((2, 24, 768), f32),
            pltpu.VMEM((2, 24, 768), f32),
            pltpu.VMEM((rows, 768), f32),
            pltpu.VMEM((64, 768), f32),
            pltpu.VMEM((HALF, 128), f32),
            pltpu.VMEM((HALF // 2, 128), f32),
            pltpu.VMEM((HALF // 2, 128), bf16),
            pltpu.VMEM((HALF // 2, 128), bf16),
            dma((7,)),
            dma((7,)),
            dma((7,)),
            dma((54,)),
            dma((54,)),
            dma((57,)),
            dma((57,)),
        ],
        compiler_params=pltpu.CompilerParams(
            collective_id=0, has_side_effects=True, vmem_limit_bytes=24 << 20
        ),
        name="exchange",
    )(ll, gl, ml, local_embed.reshape(rows, 768), global_embed, momentum_embed, bt)
    outs = pl.pallas_call(
        finish_kernel,
        out_shape=(
            *[jax.ShapeDtypeStruct(grouped, f32)] * 3,
            jax.ShapeDtypeStruct((2, 2, 2, 4, 4, 3, 8, 768), bf16),
            *[jax.ShapeDtypeStruct((rows, 768), f32)] * 3,
        ),
        in_specs=[VMEM] * 8,
        out_specs=(HBM,) * 7,
        scratch_shapes=[pltpu.VMEM(grouped, f32)] * 3 + [pltpu.VMEM((rows, 768), f32)] * 3 + [dma((4,)), dma((24,))],
        compiler_params=pltpu.CompilerParams(vmem_limit_bytes=24 << 20),
        name="finish",
    )(gathered, ge_v, me_v, low_total, layer_total, bt, gl, ml)
    layers = [a.reshape(4, 24, 768) for a in outs[:3]]
    return (*layers, outs[3].reshape(4, 768, 768), *outs[4:])


def solution(mesh):
    in_specs = (
        P("rep", None, "shard", None),
        P(None, "shard", None),
        P(None, "shard", None),
        P("rep", "shard", None),
        P("shard", None),
        P("shard", None),
        P(),
    )
    out_specs = (
        P(None, "shard", None),
        P(None, "shard", None),
        P(None, "shard", None),
        P(),
        P("shard", None),
        P("shard", None),
        P("shard", None),
    )
    return jax.shard_map(body, mesh=mesh, in_specs=in_specs, out_specs=out_specs, check_vma=False)
```

```python
import functools

import jax
import jax.numpy as jnp
from jax import lax
from jax.experimental import pallas as pl
from jax.experimental.pallas import tpu as pltpu
from jax.sharding import PartitionSpec as P

OUTER_MOMENTUM = 0.9
OUTER_RATE = 0.7
MESH = pl.DeviceIdType.MESH
HBM = pl.BlockSpec(memory_space=pltpu.HBM)
VMEM = pl.BlockSpec(memory_space=pltpu.VMEM)
X, Y, Z = 0, 1, 2
ORDERS = ((X, Y, Z), (Y, Z, X), (Z, X, Y))
DELTAS = (1, 3, 2)
HALF = 512


def outer_update(mean_diff, momentum, weights):
    new_moment = OUTER_MOMENTUM * momentum + mean_diff
    new_weights = weights - OUTER_RATE * (mean_diff + OUTER_MOMENTUM * new_moment)
    return (new_moment, new_weights)


def where_am_i():
    rep, shard = lax.axis_index("rep"), lax.axis_index("shard")
    z_low, core = lax.div(rep, 2), lax.rem(rep, 2)
    z_high, x, y = lax.div(shard, 16), lax.rem(lax.div(shard, 4), 4), lax.rem(shard, 4)
    return [x, y, z_high * 2 + z_low], core


def device(at, core):
    x, y, z = at
    return (lax.rem(z, 2) * 2 + core, lax.div(z, 2) * 16 + x * 4 + y)


def moved(at, axis, step):
    return [lax.rem(c + step, 4) if i == axis else c for i, c in enumerate(at)]


def piece(gathered, at, core, part):
    x, y, z = (slice(None) if c is None else c for c in at)
    z_low, z_high = (z, z) if isinstance(z, slice) else (lax.rem(z, 2), lax.div(z, 2))
    return gathered.at[z_low, core, z_high, x, y, part]


def exchange_kernel(
    ll, gl, ml, le, ge, me, bt,
    gathered, ge_v, me_v, low_total, layer_total, bt_v, gl_v, ml_v,
    ll_v, ll_other, part_sum, part_other, le_v, low, low_in, low_half, low_other,
    load_sem, rep_send, rep_recv, ring_send, ring_recv, pair_send, pair_recv,
):
    at, core = where_am_i()
    other = 1 - core
    z_low = lax.rem(at[Z], 2)
    twin_at = [at[X], at[Y], at[Z] + 1 - 2 * z_low]
    pair, twin = device(at, other), device(twin_at, core)
    rows = ge.shape[0]

    def remote(src, dst, sems, i, to):
        send, recv = sems
        return pltpu.make_async_remote_copy(src, dst, send.at[i], recv.at[i], device_id=to, device_id_type=MESH)

    loads = [
        pltpu.make_async_copy(ll.at[:, core], ll_v, load_sem.at[0]),
        pltpu.make_async_copy(gl, gl_v, load_sem.at[1]),
        pltpu.make_async_copy(ml, ml_v, load_sem.at[2]),
        pltpu.make_async_copy(bt, bt_v, load_sem.at[3]),
        pltpu.make_async_copy(le, le_v, load_sem.at[4]),
        pltpu.make_async_copy(ge, ge_v, load_sem.at[5]),
        pltpu.make_async_copy(me, me_v, load_sem.at[6]),
    ]
    for load in loads:
        load.start()

    barrier = pltpu.get_barrier_semaphore()
    peers = [pair] + [device(moved(at, axis, step), core) for axis in (X, Y, Z) for step in DELTAS]
    for peer in peers:
        pl.semaphore_signal(barrier, inc=1, device_id=peer, device_id_type=MESH)
    pl.semaphore_wait(barrier, len(peers))

    rep = (rep_send, rep_recv)
    to_pair = remote(ll.at[:, other], ll_other, rep, 0, pair)
    to_pair.start()
    loads[0].wait()
    loads[1].wait()
    to_pair.wait_recv()
    weights = gl_v[:, core]
    part_sum[...] = ((weights - ll_v[...]) + (weights - ll_other[...])).astype(jnp.bfloat16)
    first = remote(part_sum.at[1 - z_low], part_other.at[1 - z_low], rep, 1, twin)
    second = remote(part_sum.at[z_low], part_other.at[z_low], rep, 2, twin)
    first.start()
    second.start()

    loads[3].wait()
    loads[4].wait()
    loads[5].wait()
    basis = bt_v[...].astype(jnp.bfloat16)
    none = jnp.zeros_like(basis)
    left, right = jnp.concatenate([basis, none], 0), jnp.concatenate([none, basis], 0)
    nt = (((1,), (1,)), ((), ()))

    def local_rows(start, size):
        return jnp.concatenate([le_v[pl.ds(6 * start + c, size, 6), :] for c in range(6)], 1)

    for start in range(0, HALF, 128):
        tail = min(128, rows - HALF - start)
        a, b = pl.ds(start, 128), pl.ds(HALF + start, tail)
        da = (ge_v[a, :] - local_rows(start, 128)).astype(jnp.bfloat16)
        db = (ge_v[b, :] - local_rows(HALF + start, tail)).astype(jnp.bfloat16)
        pa = lax.dot_general(da, left, nt, preferred_element_type=jnp.float32)
        pb = lax.dot_general(db, right, nt, preferred_element_type=jnp.float32)
        low[a, :] = pa
        low[pl.ds(start, tail), :] = low[pl.ds(start, tail), :] + pb
    quarter = HALF // 2
    mine, theirs = pl.ds(core * quarter, quarter), pl.ds(other * quarter, quarter)
    low_to_pair = remote(low.at[theirs], low_in, rep, 3, pair)
    low_to_pair.start()

    loads[2].wait()
    first_in = remote(part_sum.at[z_low], part_other.at[z_low], rep, 1, twin)
    first_in.wait_recv()
    mean = (part_sum[z_low].astype(jnp.float32) + part_other[z_low].astype(jnp.float32)) / 4
    _, weights = outer_update(mean, ml_v[z_low, core], gl_v[z_low, core])
    gathered[z_low, core, lax.div(at[Z], 2), at[X], at[Y]] = weights.astype(jnp.bfloat16).reshape(3, 8, 768)

    ring, pairs = (ring_send, ring_recv), (pair_send, pair_recv)
    started, expected = [], []

    def send(where, part, slot, to):
        copy = remote(piece(gathered, where, core, part), piece(gathered, where, core, part), ring, part * 18 + slot, to)
        copy.start()
        started.append(copy)

    def arrive(where, part, slot):
        ref = piece(gathered, where, core, part)
        remote(ref, ref, ring, part * 18 + slot, pair).wait_recv()
        share(where, part, slot)

    def share(where, part, slot):
        ref = piece(gathered, where, core, part)
        copy = remote(ref, ref, pairs, part * 19 + slot, pair)
        copy.start()
        started.append(copy)
        back = piece(gathered, where, other, part)
        expected.append(remote(back, back, pairs, part * 19 + slot, pair))

    def opened(where, *axes):
        return [None if i in axes else c for i, c in enumerate(where)]

    for part, (d1, d2, d3) in enumerate(ORDERS):
        for i, step in enumerate(DELTAS):
            send(at, part, i, device(moved(at, d1, step), core))
    for part in range(3):
        share(at, part, 18)

    low_to_pair.wait_recv()
    half = low[mine, :] + low_in[...]
    low_half[...] = half.astype(jnp.bfloat16)
    low_to_twin = remote(low_half, low_other, rep, 4, twin)
    low_to_twin.start()

    for part, (d1, d2, d3) in enumerate(ORDERS):
        for i, step in enumerate(DELTAS):
            arrive(moved(at, d1, 4 - step), part, i)
        row = opened(at, d1)
        for i, step in enumerate(DELTAS):
            send(row, part, 3 + i, device(moved(at, d2, step), core))
        for i, step in enumerate((1, 3)):
            send(row, part, 6 + i, device(moved(at, d3, step), core))

    low_to_twin.wait_recv()
    low_total[mine, :] = low_half[...].astype(jnp.float32) + low_other[...].astype(jnp.float32)
    low_back = remote(low_total.at[mine], low_total.at[mine], rep, 5, pair)
    low_back.start()

    second_in = remote(part_sum.at[1 - z_low], part_other.at[1 - z_low], rep, 2, twin)
    second_in.wait_recv()
    layer_total[:, core] = part_sum[...].astype(jnp.float32) + part_other[...].astype(jnp.float32)
    total_back = remote(layer_total.at[:, core], layer_total.at[:, core], rep, 6, pair)
    total_back.start()

    for j, back in enumerate(DELTAS):
        for part, (d1, d2, d3) in enumerate(ORDERS):
            row = opened(moved(at, d2, 4 - back), d1)
            arrive(row, part, 3 + j)
            for i, step in enumerate((1, 3)):
                send(row, part, 8 + 2 * j + i, device(moved(at, d3, step), core))

    for j, back in enumerate((0,) + DELTAS):
        for part, (d1, d2, d3) in enumerate(ORDERS):
            for i, step in enumerate((1, 3)):
                row = opened(moved(moved(at, d2, 4 - back), d3, 4 - step), d1)
                arrive(row, part, 6 + 2 * j + i)
                if j // 2 == i:
                    send(row, part, 14 + j, device(moved(at, d3, step), core))
    for j, back in enumerate((0,) + DELTAS):
        for part, (d1, d2, d3) in enumerate(ORDERS):
            arrive(opened(moved(moved(at, d2, 4 - back), d3, 2), d1), part, 14 + j)

    remote(low_total.at[theirs], low_total.at[theirs], rep, 5, pair).wait_recv()
    remote(layer_total.at[:, other], layer_total.at[:, other], rep, 6, pair).wait_recv()
    for copy in expected:
        copy.wait_recv()
    for copy in started + [to_pair, first, second, low_to_pair, low_to_twin, low_back, total_back]:
        copy.wait_send()
    loads[6].wait()


def finish_kernel(
    gathered, ge_v, me_v, low_total, layer_total, bt_v, gl_v, ml_v,
    mean_l, moment_l, weights_l, copy_l, mean_e, moment_e, weights_e,
    mean_lv, moment_lv, weights_lv, mean_v, moment_v, weights_v, sem, sem_e,
):
    rows = ge_v.shape[0]
    copies = []

    def put(src, dst, s):
        copy = pltpu.make_async_copy(src, dst, s)
        copy.start()
        copies.append(copy)

    put(gathered, copy_l, sem.at[0])
    basis = bt_v[...]
    high = basis.astype(jnp.bfloat16)
    none = jnp.zeros_like(high)
    left = jnp.concatenate([high, none, high, none], 0)
    right = jnp.concatenate([none, high, none, high], 0)
    for n, start in enumerate(range(0, rows, 128)):
        size = min(128, rows - start)
        packed = low_total[pl.ds(start % HALF, size), :] / 4
        top = packed.astype(jnp.bfloat16)
        rest = (packed - top.astype(jnp.float32)).astype(jnp.bfloat16)
        at = pl.ds(start, size)
        mean = jnp.dot(
            jnp.concatenate([top, rest], 1), left if start < HALF else right, preferred_element_type=jnp.float32
        )
        moment, weights = outer_update(mean, me_v[at, :], ge_v[at, :])
        for k, (value, buf, out) in enumerate(
            ((mean, mean_v, mean_e), (moment, moment_v, moment_e), (weights, weights_v, weights_e))
        ):
            buf[at, :] = value
            put(buf.at[at], out.at[at], sem_e.at[3 * n + k])
    mean = layer_total[...] / 4
    moment, weights = outer_update(mean, ml_v[...], gl_v[...])
    for k, (value, buf, out) in enumerate(
        ((mean, mean_lv, mean_l), (moment, moment_lv, moment_l), (weights, weights_lv, weights_l))
    ):
        buf[...] = value
        put(buf, out, sem.at[1 + k])
    for copy in copies:
        copy.wait()


def body(local_layers, global_layers, momentum_layers, local_embed, global_embed, momentum_embed, proj_basis):
    rows = global_embed.shape[0]
    grouped = (2, 2, 24, 768)
    ll, gl, ml = (a.reshape(grouped) for a in (local_layers, global_layers, momentum_layers))
    bt = proj_basis.T
    f32, bf16 = jnp.float32, jnp.bfloat16
    dma = pltpu.SemaphoreType.DMA
    kept = pl.pallas_call(
        exchange_kernel,
        out_shape=(
            pltpu.VMEM((2, 2, 2, 4, 4, 3, 8, 768), bf16),
            pltpu.VMEM((rows, 768), f32),
            pltpu.VMEM((rows, 768), f32),
            pltpu.VMEM((HALF, 128), f32),
            pltpu.VMEM(grouped, f32),
            pltpu.VMEM((64, 768), f32),
            pltpu.VMEM(grouped, f32),
            pltpu.VMEM(grouped, f32),
        ),
        in_specs=[HBM] * 7,
        out_specs=(VMEM,) * 8,
        scratch_shapes=[
            pltpu.VMEM((2, 24, 768), f32),
            pltpu.VMEM((2, 24, 768), f32),
            pltpu.VMEM((2, 24, 768), bf16),
            pltpu.VMEM((2, 24, 768), bf16),
            pltpu.VMEM((rows * 6, 128), f32),
            pltpu.VMEM((HALF, 128), f32),
            pltpu.VMEM((HALF // 2, 128), f32),
            pltpu.VMEM((HALF // 2, 128), bf16),
            pltpu.VMEM((HALF // 2, 128), bf16),
            dma((7,)),
            dma((7,)),
            dma((7,)),
            dma((54,)),
            dma((54,)),
            dma((57,)),
            dma((57,)),
        ],
        compiler_params=pltpu.CompilerParams(
            collective_id=0, has_side_effects=True, vmem_limit_bytes=52 << 20
        ),
        name="exchange",
    )(ll, gl, ml, local_embed.reshape(rows * 6, 128), global_embed, momentum_embed, bt)
    outs = pl.pallas_call(
        finish_kernel,
        out_shape=(
            *[jax.ShapeDtypeStruct(grouped, f32)] * 3,
            jax.ShapeDtypeStruct((2, 2, 2, 4, 4, 3, 8, 768), bf16),
            *[jax.ShapeDtypeStruct((rows, 768), f32)] * 3,
        ),
        in_specs=[VMEM] * 8,
        out_specs=(HBM,) * 7,
        scratch_shapes=[pltpu.VMEM(grouped, f32)] * 3 + [pltpu.VMEM((rows, 768), f32)] * 3 + [dma((4,)), dma((24,))],
        compiler_params=pltpu.CompilerParams(vmem_limit_bytes=24 << 20),
        name="finish",
    )(*kept)
    layers = [a.reshape(4, 24, 768) for a in outs[:3]]
    return (*layers, outs[3].reshape(4, 768, 768), *outs[4:])


def solution(mesh):
    in_specs = (
        P("rep", None, "shard", None),
        P(None, "shard", None),
        P(None, "shard", None),
        P("rep", "shard", None),
        P("shard", None),
        P("shard", None),
        P(),
    )
    out_specs = (
        P(None, "shard", None),
        P(None, "shard", None),
        P(None, "shard", None),
        P(),
        P("shard", None),
        P("shard", None),
        P("shard", None),
    )
    return jax.shard_map(body, mesh=mesh, in_specs=in_specs, out_specs=out_specs, check_vma=False)
```

```python
import functools

import jax
import jax.numpy as jnp
from jax import lax
from jax.experimental import pallas as pl
from jax.experimental.pallas import tpu as pltpu
from jax.sharding import PartitionSpec as P

OUTER_MOMENTUM = 0.9
OUTER_RATE = 0.7
MESH = pl.DeviceIdType.MESH
HBM = pl.BlockSpec(memory_space=pltpu.HBM)
VMEM = pl.BlockSpec(memory_space=pltpu.VMEM)
X, Y, Z = 0, 1, 2
ORDERS = ((X, Y, Z), (Y, Z, X), (Z, X, Y))
DELTAS = (1, 3, 2)
HALF = 512


def outer_update(mean_diff, momentum, weights):
    new_moment = OUTER_MOMENTUM * momentum + mean_diff
    new_weights = weights - OUTER_RATE * (mean_diff + OUTER_MOMENTUM * new_moment)
    return (new_moment, new_weights)


def where_am_i():
    rep, shard = lax.axis_index("rep"), lax.axis_index("shard")
    z_low, core = lax.div(rep, 2), lax.rem(rep, 2)
    z_high, x, y = lax.div(shard, 16), lax.rem(lax.div(shard, 4), 4), lax.rem(shard, 4)
    return [x, y, z_high * 2 + z_low], core


def device(at, core):
    x, y, z = at
    return (lax.rem(z, 2) * 2 + core, lax.div(z, 2) * 16 + x * 4 + y)


def moved(at, axis, step):
    return [lax.rem(c + step, 4) if i == axis else c for i, c in enumerate(at)]


def piece(gathered, at, core, part):
    x, y, z = (slice(None) if c is None else c for c in at)
    z_low, z_high = (z, z) if isinstance(z, slice) else (lax.rem(z, 2), lax.div(z, 2))
    return gathered.at[z_low, core, z_high, x, y, part]


def exchange_kernel(
    ll, gl, ml, le, ge, me, bt,
    gathered, ge_v, me_v, low_total, layer_total, bt_v, gl_v, ml_v,
    ll_v, ll_other, part_sum, part_other, le_v, low, low_in, low_half, low_other,
    load_sem, rep_send, rep_recv, ring_send, ring_recv, pair_send, pair_recv,
):
    at, core = where_am_i()
    other = 1 - core
    z_low = lax.rem(at[Z], 2)
    twin_at = [at[X], at[Y], at[Z] + 1 - 2 * z_low]
    pair, twin = device(at, other), device(twin_at, core)
    rows = ge.shape[0]

    def remote(src, dst, sems, i, to):
        send, recv = sems
        return pltpu.make_async_remote_copy(src, dst, send.at[i], recv.at[i], device_id=to, device_id_type=MESH)

    loads = [
        pltpu.make_async_copy(ll.at[:, core], ll_v, load_sem.at[0]),
        pltpu.make_async_copy(gl, gl_v, load_sem.at[1]),
        pltpu.make_async_copy(ml, ml_v, load_sem.at[2]),
        pltpu.make_async_copy(bt, bt_v, load_sem.at[3]),
        pltpu.make_async_copy(le, le_v, load_sem.at[4]),
        pltpu.make_async_copy(ge, ge_v, load_sem.at[5]),
        pltpu.make_async_copy(me, me_v, load_sem.at[6]),
    ]
    for load in loads[:6]:
        load.start()

    barrier = pltpu.get_barrier_semaphore()
    peers = [pair] + [device(moved(at, axis, step), core) for axis in (X, Y, Z) for step in DELTAS]
    for peer in peers:
        pl.semaphore_signal(barrier, inc=1, device_id=peer, device_id_type=MESH)
    pl.semaphore_wait(barrier, len(peers))

    rep = (rep_send, rep_recv)
    to_pair = remote(ll.at[:, other], ll_other, rep, 0, pair)
    to_pair.start()
    loads[0].wait()
    loads[1].wait()
    to_pair.wait_recv()
    weights = gl_v[:, core]
    part_sum[...] = ((weights - ll_v[...]) + (weights - ll_other[...])).astype(jnp.bfloat16)
    first = remote(part_sum.at[1 - z_low], part_other.at[1 - z_low], rep, 1, twin)
    second = remote(part_sum.at[z_low], part_other.at[z_low], rep, 2, twin)
    first.start()
    second.start()

    loads[3].wait()
    loads[4].wait()
    loads[5].wait()
    loads[6].start()
    basis = bt_v[...].astype(jnp.bfloat16)
    none = jnp.zeros_like(basis)
    left, right = jnp.concatenate([basis, none], 0), jnp.concatenate([none, basis], 0)
    nt = (((1,), (1,)), ((), ()))

    def local_rows(start, size):
        return jnp.concatenate([le_v[pl.ds(6 * start + c, size, 6), :] for c in range(6)], 1)

    for start in range(0, HALF, 128):
        tail = min(128, rows - HALF - start)
        a, b = pl.ds(start, 128), pl.ds(HALF + start, tail)
        da = (ge_v[a, :] - local_rows(start, 128)).astype(jnp.bfloat16)
        db = (ge_v[b, :] - local_rows(HALF + start, tail)).astype(jnp.bfloat16)
        pa = lax.dot_general(da, left, nt, preferred_element_type=jnp.float32)
        pb = lax.dot_general(db, right, nt, preferred_element_type=jnp.float32)
        low[a, :] = pa
        low[pl.ds(start, tail), :] = low[pl.ds(start, tail), :] + pb
    quarter = HALF // 2
    mine, theirs = pl.ds(core * quarter, quarter), pl.ds(other * quarter, quarter)
    low_to_pair = remote(low.at[theirs], low_in, rep, 3, pair)
    low_to_pair.start()

    loads[2].wait()
    first_in = remote(part_sum.at[z_low], part_other.at[z_low], rep, 1, twin)
    first_in.wait_recv()
    mean = (part_sum[z_low].astype(jnp.float32) + part_other[z_low].astype(jnp.float32)) / 4
    _, weights = outer_update(mean, ml_v[z_low, core], gl_v[z_low, core])
    gathered[z_low, core, lax.div(at[Z], 2), at[X], at[Y]] = weights.astype(jnp.bfloat16).reshape(3, 8, 768)

    ring, pairs = (ring_send, ring_recv), (pair_send, pair_recv)
    started, expected = [], []

    def send(where, part, slot, to):
        copy = remote(piece(gathered, where, core, part), piece(gathered, where, core, part), ring, part * 27 + slot, to)
        copy.start()
        started.append(copy)

    def arrive(where, part, slot):
        ref = piece(gathered, where, core, part)
        remote(ref, ref, ring, part * 27 + slot, pair).wait_recv()

    def share(where, part, slot):
        ref = piece(gathered, where, core, part)
        copy = remote(ref, ref, pairs, part * 19 + slot, pair)
        copy.start()
        started.append(copy)
        back = piece(gathered, where, other, part)
        expected.append(remote(back, back, pairs, part * 19 + slot, pair))

    def opened(where, *axes):
        return [None if i in axes else c for i, c in enumerate(where)]

    for part, (d1, d2, d3) in enumerate(ORDERS):
        for i, step in enumerate(DELTAS):
            send(at, part, i, device(moved(at, d1, step), core))
    for part, (d1, d2, d3) in enumerate(ORDERS):
        for j, step in enumerate(DELTAS):
            send(at, part, 3 + 4 * j, device(moved(at, d2, step), core))
    for part in range(3):
        share(at, part, 18)

    low_to_pair.wait_recv()
    half = low[mine, :] + low_in[...]
    low_half[...] = half.astype(jnp.bfloat16)
    low_to_twin = remote(low_half, low_other, rep, 4, twin)
    low_to_twin.start()

    for i, back in enumerate(DELTAS):
        for part, (d1, d2, d3) in enumerate(ORDERS):
            chunk = moved(at, d1, 4 - back)
            arrive(chunk, part, i)
            for j, step in enumerate(DELTAS):
                send(chunk, part, 4 + 4 * j + i, device(moved(at, d2, step), core))
            share(chunk, part, i)
    for part, (d1, d2, d3) in enumerate(ORDERS):
        for i, step in enumerate((1, 3)):
            send(opened(at, d1), part, 15 + i, device(moved(at, d3, step), core))

    for j, back in enumerate(DELTAS):
        for part, (d1, d2, d3) in enumerate(ORDERS):
            first_chunk = moved(at, d2, 4 - back)
            for k, across in enumerate((0,) + DELTAS):
                arrive(moved(first_chunk, d1, 4 - across), part, 3 + 4 * j + k)
            row = opened(first_chunk, d1)
            for i, step in enumerate((1, 3)):
                send(row, part, 17 + 2 * j + i, device(moved(at, d3, step), core))
            share(row, part, 3 + j)

    low_to_twin.wait_recv()
    low_total[mine, :] = low_half[...].astype(jnp.float32) + low_other[...].astype(jnp.float32)
    low_back = remote(low_total.at[mine], low_total.at[mine], rep, 5, pair)
    low_back.start()

    second_in = remote(part_sum.at[1 - z_low], part_other.at[1 - z_low], rep, 2, twin)
    second_in.wait_recv()
    layer_total[:, core] = part_sum[...].astype(jnp.float32) + part_other[...].astype(jnp.float32)
    total_back = remote(layer_total.at[:, core], layer_total.at[:, core], rep, 6, pair)
    total_back.start()

    for j, back in enumerate((0,) + DELTAS):
        for part, (d1, d2, d3) in enumerate(ORDERS):
            for i, step in enumerate((1, 3)):
                row = opened(moved(moved(at, d2, 4 - back), d3, 4 - step), d1)
                arrive(row, part, 15 + 2 * j + i)
                if j // 2 == i:
                    send(row, part, 23 + j, device(moved(at, d3, step), core))
                share(row, part, 6 + 2 * j + i)
    for j, back in enumerate((0,) + DELTAS):
        for part, (d1, d2, d3) in enumerate(ORDERS):
            row = opened(moved(moved(at, d2, 4 - back), d3, 2), d1)
            arrive(row, part, 23 + j)
            share(row, part, 14 + j)

    remote(low_total.at[theirs], low_total.at[theirs], rep, 5, pair).wait_recv()
    remote(layer_total.at[:, other], layer_total.at[:, other], rep, 6, pair).wait_recv()
    for copy in expected:
        copy.wait_recv()
    for copy in started + [to_pair, first, second, low_to_pair, low_to_twin, low_back, total_back]:
        copy.wait_send()
    loads[6].wait()


def finish_kernel(
    gathered, ge_v, me_v, low_total, layer_total, bt_v, gl_v, ml_v,
    mean_l, moment_l, weights_l, copy_l, mean_e, moment_e, weights_e,
    mean_lv, moment_lv, weights_lv, mean_v, moment_v, weights_v, sem, sem_e,
):
    rows = ge_v.shape[0]
    copies = []

    def put(src, dst, s):
        copy = pltpu.make_async_copy(src, dst, s)
        copy.start()
        copies.append(copy)

    put(gathered, copy_l, sem.at[0])
    basis = bt_v[...]
    high = basis.astype(jnp.bfloat16)
    none = jnp.zeros_like(high)
    left = jnp.concatenate([high, none, high, none], 0)
    right = jnp.concatenate([none, high, none, high], 0)
    for n, start in enumerate(range(0, rows, 128)):
        size = min(128, rows - start)
        packed = low_total[pl.ds(start % HALF, size), :] / 4
        top = packed.astype(jnp.bfloat16)
        rest = (packed - top.astype(jnp.float32)).astype(jnp.bfloat16)
        at = pl.ds(start, size)
        mean = jnp.dot(
            jnp.concatenate([top, rest], 1), left if start < HALF else right, preferred_element_type=jnp.float32
        )
        moment, weights = outer_update(mean, me_v[at, :], ge_v[at, :])
        for k, (value, buf, out) in enumerate(
            ((mean, mean_v, mean_e), (moment, moment_v, moment_e), (weights, weights_v, weights_e))
        ):
            buf[at, :] = value
            put(buf.at[at], out.at[at], sem_e.at[3 * n + k])
    mean = layer_total[...] / 4
    moment, weights = outer_update(mean, ml_v[...], gl_v[...])
    for k, (value, buf, out) in enumerate(
        ((mean, mean_lv, mean_l), (moment, moment_lv, moment_l), (weights, weights_lv, weights_l))
    ):
        buf[...] = value
        put(buf, out, sem.at[1 + k])
    for copy in copies:
        copy.wait()


def body(local_layers, global_layers, momentum_layers, local_embed, global_embed, momentum_embed, proj_basis):
    rows = global_embed.shape[0]
    grouped = (2, 2, 24, 768)
    ll, gl, ml = (a.reshape(grouped) for a in (local_layers, global_layers, momentum_layers))
    bt = proj_basis.T
    f32, bf16 = jnp.float32, jnp.bfloat16
    dma = pltpu.SemaphoreType.DMA
    kept = pl.pallas_call(
        exchange_kernel,
        out_shape=(
            pltpu.VMEM((2, 2, 2, 4, 4, 3, 8, 768), bf16),
            pltpu.VMEM((rows, 768), f32),
            pltpu.VMEM((rows, 768), f32),
            pltpu.VMEM((HALF, 128), f32),
            pltpu.VMEM(grouped, f32),
            pltpu.VMEM((64, 768), f32),
            pltpu.VMEM(grouped, f32),
            pltpu.VMEM(grouped, f32),
        ),
        in_specs=[HBM] * 7,
        out_specs=(VMEM,) * 8,
        scratch_shapes=[
            pltpu.VMEM((2, 24, 768), f32),
            pltpu.VMEM((2, 24, 768), f32),
            pltpu.VMEM((2, 24, 768), bf16),
            pltpu.VMEM((2, 24, 768), bf16),
            pltpu.VMEM((rows * 6, 128), f32),
            pltpu.VMEM((HALF, 128), f32),
            pltpu.VMEM((HALF // 2, 128), f32),
            pltpu.VMEM((HALF // 2, 128), bf16),
            pltpu.VMEM((HALF // 2, 128), bf16),
            dma((7,)),
            dma((7,)),
            dma((7,)),
            dma((81,)),
            dma((81,)),
            dma((57,)),
            dma((57,)),
        ],
        compiler_params=pltpu.CompilerParams(
            collective_id=0, has_side_effects=True, vmem_limit_bytes=52 << 20
        ),
        name="exchange",
    )(ll, gl, ml, local_embed.reshape(rows * 6, 128), global_embed, momentum_embed, bt)
    outs = pl.pallas_call(
        finish_kernel,
        out_shape=(
            *[jax.ShapeDtypeStruct(grouped, f32)] * 3,
            jax.ShapeDtypeStruct((2, 2, 2, 4, 4, 3, 8, 768), bf16),
            *[jax.ShapeDtypeStruct((rows, 768), f32)] * 3,
        ),
        in_specs=[VMEM] * 8,
        out_specs=(HBM,) * 7,
        scratch_shapes=[pltpu.VMEM(grouped, f32)] * 3 + [pltpu.VMEM((rows, 768), f32)] * 3 + [dma((4,)), dma((24,))],
        compiler_params=pltpu.CompilerParams(vmem_limit_bytes=24 << 20),
        name="finish",
    )(*kept)
    layers = [a.reshape(4, 24, 768) for a in outs[:3]]
    return (*layers, outs[3].reshape(4, 768, 768), *outs[4:])


def solution(mesh):
    in_specs = (
        P("rep", None, "shard", None),
        P(None, "shard", None),
        P(None, "shard", None),
        P("rep", "shard", None),
        P("shard", None),
        P("shard", None),
        P(),
    )
    out_specs = (
        P(None, "shard", None),
        P(None, "shard", None),
        P(None, "shard", None),
        P(),
        P("shard", None),
        P("shard", None),
        P("shard", None),
    )
    return jax.shard_map(body, mesh=mesh, in_specs=in_specs, out_specs=out_specs, check_vma=False)
```

```python
import functools

import jax
import jax.numpy as jnp
from jax import lax
from jax.experimental import pallas as pl
from jax.experimental.pallas import tpu as pltpu
from jax.sharding import PartitionSpec as P

OUTER_MOMENTUM = 0.9
OUTER_RATE = 0.7
MESH = pl.DeviceIdType.MESH
HBM = pl.BlockSpec(memory_space=pltpu.HBM)
VMEM = pl.BlockSpec(memory_space=pltpu.VMEM)
X, Y, Z = 0, 1, 2
ORDERS = ((X, Y, Z), (Y, Z, X), (Z, X, Y))
DELTAS = (1, 3, 2)
HALF = 512


def outer_update(mean_diff, momentum, weights):
    new_moment = OUTER_MOMENTUM * momentum + mean_diff
    new_weights = weights - OUTER_RATE * (mean_diff + OUTER_MOMENTUM * new_moment)
    return (new_moment, new_weights)


def where_am_i():
    rep, shard = lax.axis_index("rep"), lax.axis_index("shard")
    z_low, core = lax.div(rep, 2), lax.rem(rep, 2)
    z_high, x, y = lax.div(shard, 16), lax.rem(lax.div(shard, 4), 4), lax.rem(shard, 4)
    return [x, y, z_high * 2 + z_low], core


def device(at, core):
    x, y, z = at
    return (lax.rem(z, 2) * 2 + core, lax.div(z, 2) * 16 + x * 4 + y)


def moved(at, axis, step):
    return [lax.rem(c + step, 4) if i == axis else c for i, c in enumerate(at)]


def piece(gathered, at, core, part):
    x, y, z = (slice(None) if c is None else c for c in at)
    z_low, z_high = (z, z) if isinstance(z, slice) else (lax.rem(z, 2), lax.div(z, 2))
    return gathered.at[z_low, core, z_high, x, y, part]


def exchange_kernel(
    ll, gl, ml, le, ge, me, bt,
    gathered, ge_v, me_v, low_total, layer_total, bt_v, gl_v, ml_v,
    ll_v, ll_other, part_sum, part_other, le_v, low, low_in, low_half, low_other,
    load_sem, rep_send, rep_recv, ring_send, ring_recv, pair_send, pair_recv,
):
    at, core = where_am_i()
    other = 1 - core
    z_low = lax.rem(at[Z], 2)
    twin_at = [at[X], at[Y], at[Z] + 1 - 2 * z_low]
    pair, twin = device(at, other), device(twin_at, core)
    rows = ge.shape[0]

    def remote(src, dst, sems, i, to):
        send, recv = sems
        return pltpu.make_async_remote_copy(src, dst, send.at[i], recv.at[i], device_id=to, device_id_type=MESH)

    loads = [
        pltpu.make_async_copy(ll, ll_v, load_sem.at[0]),
        pltpu.make_async_copy(gl, gl_v, load_sem.at[1]),
        pltpu.make_async_copy(ml, ml_v, load_sem.at[2]),
        pltpu.make_async_copy(bt, bt_v, load_sem.at[3]),
        pltpu.make_async_copy(le, le_v, load_sem.at[4]),
        pltpu.make_async_copy(ge, ge_v, load_sem.at[5]),
        pltpu.make_async_copy(me, me_v, load_sem.at[6]),
    ]
    for load in loads[:4]:
        load.start()

    barrier = pltpu.get_barrier_semaphore()
    peers = [pair] + [device(moved(at, axis, step), core) for axis in (X, Y, Z) for step in DELTAS]
    for peer in peers:
        pl.semaphore_signal(barrier, inc=1, device_id=peer, device_id_type=MESH)
    loads[0].wait()
    loads[4].start()
    loads[5].start()
    pl.semaphore_wait(barrier, len(peers))

    rep = (rep_send, rep_recv)
    to_pair = remote(ll_v.at[:, other], ll_other, rep, 0, pair)
    to_pair.start()
    loads[1].wait()
    to_pair.wait_recv()
    weights = gl_v[:, core]
    part_sum[...] = ((weights - ll_v[:, core]) + (weights - ll_other[...])).astype(jnp.bfloat16)
    first = remote(part_sum.at[1 - z_low], part_other.at[1 - z_low], rep, 1, twin)
    second = remote(part_sum.at[z_low], part_other.at[z_low], rep, 2, twin)
    first.start()
    second.start()

    loads[3].wait()
    loads[4].wait()
    loads[5].wait()
    loads[6].start()
    basis = bt_v[...].astype(jnp.bfloat16)
    none = jnp.zeros_like(basis)
    left, right = jnp.concatenate([basis, none], 0), jnp.concatenate([none, basis], 0)
    nt = (((1,), (1,)), ((), ()))

    def local_rows(start, size):
        return jnp.concatenate([le_v[pl.ds(6 * start + c, size, 6), :] for c in range(6)], 1)

    def low_rank(start):
        tail = min(128, rows - HALF - start)
        a, b = pl.ds(start, 128), pl.ds(HALF + start, tail)
        da = (ge_v[a, :] - local_rows(start, 128)).astype(jnp.bfloat16)
        db = (ge_v[b, :] - local_rows(HALF + start, tail)).astype(jnp.bfloat16)
        pa = lax.dot_general(da, left, nt, preferred_element_type=jnp.float32)
        pb = lax.dot_general(db, right, nt, preferred_element_type=jnp.float32)
        low[a, :] = pa
        low[pl.ds(start, tail), :] = low[pl.ds(start, tail), :] + pb
    for start in range(0, HALF // 2, 128):
        low_rank(start)

    loads[2].wait()
    first_in = remote(part_sum.at[z_low], part_other.at[z_low], rep, 1, twin)
    first_in.wait_recv()
    mean = (part_sum[z_low].astype(jnp.float32) + part_other[z_low].astype(jnp.float32)) / 4
    _, weights = outer_update(mean, ml_v[z_low, core], gl_v[z_low, core])
    gathered[z_low, core, lax.div(at[Z], 2), at[X], at[Y]] = weights.astype(jnp.bfloat16).reshape(3, 8, 768)

    ring, pairs = (ring_send, ring_recv), (pair_send, pair_recv)
    started, expected = [], []

    def send(where, part, slot, to):
        copy = remote(piece(gathered, where, core, part), piece(gathered, where, core, part), ring, part * 27 + slot, to)
        copy.start()
        started.append(copy)

    def arrive(where, part, slot):
        ref = piece(gathered, where, core, part)
        remote(ref, ref, ring, part * 27 + slot, pair).wait_recv()

    def share(where, part, slot):
        ref = piece(gathered, where, core, part)
        copy = remote(ref, ref, pairs, part * 19 + slot, pair)
        copy.start()
        started.append(copy)
        back = piece(gathered, where, other, part)
        expected.append(remote(back, back, pairs, part * 19 + slot, pair))

    def opened(where, *axes):
        return [None if i in axes else c for i, c in enumerate(where)]

    for part, (d1, d2, d3) in enumerate(ORDERS):
        for i, step in enumerate(DELTAS):
            send(at, part, i, device(moved(at, d1, step), core))
    for part, (d1, d2, d3) in enumerate(ORDERS):
        for j, step in enumerate((1, 3)):
            send(at, part, 3 + 4 * j, device(moved(at, d2, step), core))
    for part in range(3):
        share(at, part, 18)

    for start in range(HALF // 2, HALF, 128):
        low_rank(start)
    quarter = HALF // 2
    mine, theirs = pl.ds(core * quarter, quarter), pl.ds(other * quarter, quarter)
    low_to_pair = remote(low.at[theirs], low_in, rep, 3, pair)
    low_to_pair.start()
    low_to_pair.wait_recv()
    half = low[mine, :] + low_in[...]
    low_half[...] = half.astype(jnp.bfloat16)
    low_to_twin = remote(low_half, low_other, rep, 4, twin)
    low_to_twin.start()

    for i, back in enumerate(DELTAS):
        for part, (d1, d2, d3) in enumerate(ORDERS):
            chunk = moved(at, d1, 4 - back)
            arrive(chunk, part, i)
            for j, step in enumerate((1, 3)):
                send(chunk, part, 4 + 4 * j + i, device(moved(at, d2, step), core))
            share(chunk, part, i)
    for part, (d1, d2, d3) in enumerate(ORDERS):
        for i, step in enumerate((1, 3)):
            send(opened(at, d1), part, 15 + i, device(moved(at, d3, step), core))

    for j, back in enumerate(DELTAS):
        for part, (d1, d2, d3) in enumerate(ORDERS):
            first_chunk = moved(at, d2, 4 - back)
            for k, across in enumerate((0,) + DELTAS):
                chunk = moved(first_chunk, d1, 4 - across)
                arrive(chunk, part, 3 + 4 * j + k)
                if j == k // 2:
                    send(chunk, part, 11 + k, device(moved(at, d2, back), core))
            row = opened(first_chunk, d1)
            for i, step in enumerate((1, 3)):
                send(row, part, 17 + 2 * j + i, device(moved(at, d3, step), core))
            share(row, part, 3 + j)

    low_to_twin.wait_recv()
    low_total[mine, :] = low_half[...].astype(jnp.float32) + low_other[...].astype(jnp.float32)
    low_back = remote(low_total.at[mine], low_total.at[mine], rep, 5, pair)
    low_back.start()

    second_in = remote(part_sum.at[1 - z_low], part_other.at[1 - z_low], rep, 2, twin)
    second_in.wait_recv()
    layer_total[:, core] = part_sum[...].astype(jnp.float32) + part_other[...].astype(jnp.float32)
    total_back = remote(layer_total.at[:, core], layer_total.at[:, core], rep, 6, pair)
    total_back.start()

    for j, back in enumerate((0,) + DELTAS):
        for part, (d1, d2, d3) in enumerate(ORDERS):
            for i, step in enumerate((1, 3)):
                row = opened(moved(moved(at, d2, 4 - back), d3, 4 - step), d1)
                arrive(row, part, 15 + 2 * j + i)
                if j // 2 == i:
                    send(row, part, 23 + j, device(moved(at, d3, step), core))
                share(row, part, 6 + 2 * j + i)
    for j, back in enumerate((0,) + DELTAS):
        for part, (d1, d2, d3) in enumerate(ORDERS):
            row = opened(moved(moved(at, d2, 4 - back), d3, 2), d1)
            arrive(row, part, 23 + j)
            share(row, part, 14 + j)

    remote(low_total.at[theirs], low_total.at[theirs], rep, 5, pair).wait_recv()
    remote(layer_total.at[:, other], layer_total.at[:, other], rep, 6, pair).wait_recv()
    for copy in expected:
        copy.wait_recv()
    for copy in started + [to_pair, first, second, low_to_pair, low_to_twin, low_back, total_back]:
        copy.wait_send()
    loads[6].wait()


def finish_kernel(
    gathered, ge_v, me_v, low_total, layer_total, bt_v, gl_v, ml_v,
    mean_l, moment_l, weights_l, copy_l, mean_e, moment_e, weights_e,
    mean_lv, moment_lv, weights_lv, mean_v, moment_v, weights_v, sem, sem_e,
):
    rows = ge_v.shape[0]
    copies = []

    def put(src, dst, s):
        copy = pltpu.make_async_copy(src, dst, s)
        copy.start()
        copies.append(copy)

    put(gathered, copy_l, sem.at[0])
    basis = bt_v[...]
    high = basis.astype(jnp.bfloat16)
    none = jnp.zeros_like(high)
    left = jnp.concatenate([high, none, high, none], 0)
    right = jnp.concatenate([none, high, none, high], 0)
    for n, start in enumerate(range(0, rows, 128)):
        size = min(128, rows - start)
        packed = low_total[pl.ds(start % HALF, size), :] / 4
        top = packed.astype(jnp.bfloat16)
        rest = (packed - top.astype(jnp.float32)).astype(jnp.bfloat16)
        at = pl.ds(start, size)
        mean = jnp.dot(
            jnp.concatenate([top, rest], 1), left if start < HALF else right, preferred_element_type=jnp.float32
        )
        moment, weights = outer_update(mean, me_v[at, :], ge_v[at, :])
        for k, (value, buf, out) in enumerate(
            ((mean, mean_v, mean_e), (moment, moment_v, moment_e), (weights, weights_v, weights_e))
        ):
            buf[at, :] = value
            put(buf.at[at], out.at[at], sem_e.at[3 * n + k])
    mean = layer_total[...] / 4
    moment, weights = outer_update(mean, ml_v[...], gl_v[...])
    for k, (value, buf, out) in enumerate(
        ((mean, mean_lv, mean_l), (moment, moment_lv, moment_l), (weights, weights_lv, weights_l))
    ):
        buf[...] = value
        put(buf, out, sem.at[1 + k])
    for copy in copies:
        copy.wait()


def body(local_layers, global_layers, momentum_layers, local_embed, global_embed, momentum_embed, proj_basis):
    rows = global_embed.shape[0]
    grouped = (2, 2, 24, 768)
    ll, gl, ml = (a.reshape(grouped) for a in (local_layers, global_layers, momentum_layers))
    bt = proj_basis.T
    f32, bf16 = jnp.float32, jnp.bfloat16
    dma = pltpu.SemaphoreType.DMA
    kept = pl.pallas_call(
        exchange_kernel,
        out_shape=(
            pltpu.VMEM((2, 2, 2, 4, 4, 3, 8, 768), bf16),
            pltpu.VMEM((rows, 768), f32),
            pltpu.VMEM((rows, 768), f32),
            pltpu.VMEM((HALF, 128), f32),
            pltpu.VMEM(grouped, f32),
            pltpu.VMEM((64, 768), f32),
            pltpu.VMEM(grouped, f32),
            pltpu.VMEM(grouped, f32),
        ),
        in_specs=[HBM] * 7,
        out_specs=(VMEM,) * 8,
        scratch_shapes=[
            pltpu.VMEM(grouped, f32),
            pltpu.VMEM((2, 24, 768), f32),
            pltpu.VMEM((2, 24, 768), bf16),
            pltpu.VMEM((2, 24, 768), bf16),
            pltpu.VMEM((rows * 6, 128), f32),
            pltpu.VMEM((HALF, 128), f32),
            pltpu.VMEM((HALF // 2, 128), f32),
            pltpu.VMEM((HALF // 2, 128), bf16),
            pltpu.VMEM((HALF // 2, 128), bf16),
            dma((7,)),
            dma((7,)),
            dma((7,)),
            dma((81,)),
            dma((81,)),
            dma((57,)),
            dma((57,)),
        ],
        compiler_params=pltpu.CompilerParams(
            collective_id=0, has_side_effects=True, vmem_limit_bytes=52 << 20
        ),
        name="exchange",
    )(ll, gl, ml, local_embed.reshape(rows * 6, 128), global_embed, momentum_embed, bt)
    outs = pl.pallas_call(
        finish_kernel,
        out_shape=(
            *[jax.ShapeDtypeStruct(grouped, f32)] * 3,
            jax.ShapeDtypeStruct((2, 2, 2, 4, 4, 3, 8, 768), bf16),
            *[jax.ShapeDtypeStruct((rows, 768), f32)] * 3,
        ),
        in_specs=[VMEM] * 8,
        out_specs=(HBM,) * 7,
        scratch_shapes=[pltpu.VMEM(grouped, f32)] * 3 + [pltpu.VMEM((rows, 768), f32)] * 3 + [dma((4,)), dma((24,))],
        compiler_params=pltpu.CompilerParams(vmem_limit_bytes=24 << 20),
        name="finish",
    )(*kept)
    layers = [a.reshape(4, 24, 768) for a in outs[:3]]
    return (*layers, outs[3].reshape(4, 768, 768), *outs[4:])


def solution(mesh):
    in_specs = (
        P("rep", None, "shard", None),
        P(None, "shard", None),
        P(None, "shard", None),
        P("rep", "shard", None),
        P("shard", None),
        P("shard", None),
        P(),
    )
    out_specs = (
        P(None, "shard", None),
        P(None, "shard", None),
        P(None, "shard", None),
        P(),
        P("shard", None),
        P("shard", None),
        P("shard", None),
    )
    return jax.shard_map(body, mesh=mesh, in_specs=in_specs, out_specs=out_specs, check_vma=False)
```

```python
import functools

import jax
import jax.numpy as jnp
from jax import lax
from jax.experimental import pallas as pl
from jax.experimental.pallas import tpu as pltpu
from jax.sharding import PartitionSpec as P

OUTER_MOMENTUM = 0.9
OUTER_RATE = 0.7
MESH = pl.DeviceIdType.MESH
HBM = pl.BlockSpec(memory_space=pltpu.HBM)
VMEM = pl.BlockSpec(memory_space=pltpu.VMEM)
X, Y, Z = 0, 1, 2
ORDERS = ((X, Y, Z), (Y, Z, X), (Z, X, Y))
DELTAS = (1, 3, 2)
HALF = 512


def outer_update(mean_diff, momentum, weights):
    new_moment = OUTER_MOMENTUM * momentum + mean_diff
    new_weights = weights - OUTER_RATE * (mean_diff + OUTER_MOMENTUM * new_moment)
    return (new_moment, new_weights)


def where_am_i():
    rep, shard = lax.axis_index("rep"), lax.axis_index("shard")
    z_low, core = lax.div(rep, 2), lax.rem(rep, 2)
    z_high, x, y = lax.div(shard, 16), lax.rem(lax.div(shard, 4), 4), lax.rem(shard, 4)
    return [x, y, z_high * 2 + z_low], core


def device(at, core):
    x, y, z = at
    return (lax.rem(z, 2) * 2 + core, lax.div(z, 2) * 16 + x * 4 + y)


def moved(at, axis, step):
    return [lax.rem(c + step, 4) if i == axis else c for i, c in enumerate(at)]


def piece(gathered, at, core, part):
    x, y, z = (slice(None) if c is None else c for c in at)
    z_low, z_high = (z, z) if isinstance(z, slice) else (lax.rem(z, 2), lax.div(z, 2))
    return gathered.at[z_low, core, z_high, x, y, part]


def exchange_kernel(
    ll, gl, ml, le, ge, me, bt,
    gathered, ge_v, me_v, low_total, layer_total, bt_v, gl_v, ml_v,
    ll_v, ll_other, part_sum, part_other, le_v, low, low_in, low_half, low_other,
    load_sem, rep_send, rep_recv, ring_send, ring_recv, pair_send, pair_recv,
):
    at, core = where_am_i()
    other = 1 - core
    z_low = lax.rem(at[Z], 2)
    twin_at = [at[X], at[Y], at[Z] + 1 - 2 * z_low]
    pair, twin = device(at, other), device(twin_at, core)
    rows = ge.shape[0]

    def remote(src, dst, sems, i, to):
        send, recv = sems
        return pltpu.make_async_remote_copy(src, dst, send.at[i], recv.at[i], device_id=to, device_id_type=MESH)

    loads = [
        pltpu.make_async_copy(ll.at[:, core], ll_v, load_sem.at[0]),
        pltpu.make_async_copy(gl, gl_v, load_sem.at[1]),
        pltpu.make_async_copy(ml, ml_v, load_sem.at[2]),
        pltpu.make_async_copy(bt, bt_v, load_sem.at[3]),
        pltpu.make_async_copy(le, le_v, load_sem.at[4]),
        pltpu.make_async_copy(ge, ge_v, load_sem.at[5]),
        pltpu.make_async_copy(me, me_v, load_sem.at[6]),
    ]
    for load in loads[:6]:
        load.start()

    barrier = pltpu.get_barrier_semaphore()
    peers = [pair] + [device(moved(at, axis, step), core) for axis in (X, Y, Z) for step in DELTAS]
    for peer in peers:
        pl.semaphore_signal(barrier, inc=1, device_id=peer, device_id_type=MESH)
    pl.semaphore_wait(barrier, len(peers))

    rep = (rep_send, rep_recv)
    to_pair = remote(ll.at[:, other], ll_other, rep, 0, pair)
    to_pair.start()
    loads[0].wait()
    loads[1].wait()
    to_pair.wait_recv()
    weights = gl_v[:, core]
    part_sum[...] = ((weights - ll_v[...]) + (weights - ll_other[...])).astype(jnp.bfloat16)
    first = remote(part_sum.at[1 - z_low], part_other.at[1 - z_low], rep, 1, twin)
    second = remote(part_sum.at[z_low], part_other.at[z_low], rep, 2, twin)
    first.start()
    second.start()

    loads[3].wait()
    loads[4].wait()
    loads[5].wait()
    loads[6].start()
    basis = bt_v[...].astype(jnp.bfloat16)
    none = jnp.zeros_like(basis)
    left, right = jnp.concatenate([basis, none], 0), jnp.concatenate([none, basis], 0)
    nt = (((1,), (1,)), ((), ()))

    def local_rows(start, size):
        return jnp.concatenate([le_v[pl.ds(6 * start + c, size, 6), :] for c in range(6)], 1)

    for start in range(0, HALF, 128):
        tail = min(128, rows - HALF - start)
        a, b = pl.ds(start, 128), pl.ds(HALF + start, tail)
        da = (ge_v[a, :] - local_rows(start, 128)).astype(jnp.bfloat16)
        db = (ge_v[b, :] - local_rows(HALF + start, tail)).astype(jnp.bfloat16)
        pa = lax.dot_general(da, left, nt, preferred_element_type=jnp.float32)
        pb = lax.dot_general(db, right, nt, preferred_element_type=jnp.float32)
        low[a, :] = pa
        low[pl.ds(start, tail), :] = low[pl.ds(start, tail), :] + pb
    quarter = HALF // 2
    mine, theirs = pl.ds(core * quarter, quarter), pl.ds(other * quarter, quarter)
    low_to_pair = remote(low.at[theirs], low_in, rep, 3, pair)
    low_to_pair.start()

    loads[2].wait()
    first_in = remote(part_sum.at[z_low], part_other.at[z_low], rep, 1, twin)
    first_in.wait_recv()
    mean = (part_sum[z_low].astype(jnp.float32) + part_other[z_low].astype(jnp.float32)) / 4
    _, weights = outer_update(mean, ml_v[z_low, core], gl_v[z_low, core])
    gathered[z_low, core, lax.div(at[Z], 2), at[X], at[Y]] = weights.astype(jnp.bfloat16).reshape(3, 8, 768)

    ring, pairs = (ring_send, ring_recv), (pair_send, pair_recv)
    started, expected = [], []

    def send(where, part, slot, to):
        copy = remote(piece(gathered, where, core, part), piece(gathered, where, core, part), ring, part * 27 + slot, to)
        copy.start()
        started.append(copy)

    def arrive(where, part, slot):
        ref = piece(gathered, where, core, part)
        remote(ref, ref, ring, part * 27 + slot, pair).wait_recv()

    def share(where, part, slot):
        ref = piece(gathered, where, core, part)
        copy = remote(ref, ref, pairs, part * 19 + slot, pair)
        copy.start()
        started.append(copy)
        back = piece(gathered, where, other, part)
        expected.append(remote(back, back, pairs, part * 19 + slot, pair))

    def opened(where, *axes):
        return [None if i in axes else c for i, c in enumerate(where)]

    for part, (d1, d2, d3) in enumerate(ORDERS):
        for i, step in enumerate(DELTAS):
            send(at, part, i, device(moved(at, d1, step), core))
    for part, (d1, d2, d3) in enumerate(ORDERS):
        for j, step in enumerate((1, 3)):
            send(at, part, 3 + 4 * j, device(moved(at, d2, step), core))
    for part in range(3):
        share(at, part, 18)

    for i, back in enumerate(DELTAS):
        for part, (d1, d2, d3) in enumerate(ORDERS):
            chunk = moved(at, d1, 4 - back)
            arrive(chunk, part, i)
            for j, step in enumerate((1, 3)):
                send(chunk, part, 4 + 4 * j + i, device(moved(at, d2, step), core))
            share(chunk, part, i)
    for part, (d1, d2, d3) in enumerate(ORDERS):
        for i, step in enumerate((1, 3)):
            send(opened(at, d1), part, 15 + i, device(moved(at, d3, step), core))

    low_to_pair.wait_recv()
    half = low[mine, :] + low_in[...]
    low_half[...] = half.astype(jnp.bfloat16)
    low_to_twin = remote(low_half, low_other, rep, 4, twin)
    low_to_twin.start()

    for j, back in enumerate(DELTAS):
        for part, (d1, d2, d3) in enumerate(ORDERS):
            first_chunk = moved(at, d2, 4 - back)
            for k, across in enumerate((0,) + DELTAS):
                chunk = moved(first_chunk, d1, 4 - across)
                arrive(chunk, part, 3 + 4 * j + k)
                if j == k // 2:
                    send(chunk, part, 11 + k, device(moved(at, d2, back), core))
            row = opened(first_chunk, d1)
            for i, step in enumerate((1, 3)):
                send(row, part, 17 + 2 * j + i, device(moved(at, d3, step), core))
            share(row, part, 3 + j)

    low_to_twin.wait_recv()
    low_total[mine, :] = low_half[...].astype(jnp.float32) + low_other[...].astype(jnp.float32)
    low_back = remote(low_total.at[mine], low_total.at[mine], rep, 5, pair)
    low_back.start()

    second_in = remote(part_sum.at[1 - z_low], part_other.at[1 - z_low], rep, 2, twin)
    second_in.wait_recv()
    layer_total[:, core] = part_sum[...].astype(jnp.float32) + part_other[...].astype(jnp.float32)
    total_back = remote(layer_total.at[:, core], layer_total.at[:, core], rep, 6, pair)
    total_back.start()

    for j, back in enumerate((0,) + DELTAS):
        for part, (d1, d2, d3) in enumerate(ORDERS):
            for i, step in enumerate((1, 3)):
                row = opened(moved(moved(at, d2, 4 - back), d3, 4 - step), d1)
                arrive(row, part, 15 + 2 * j + i)
                if j // 2 == i:
                    send(row, part, 23 + j, device(moved(at, d3, step), core))
                share(row, part, 6 + 2 * j + i)
    for j, back in enumerate((0,) + DELTAS):
        for part, (d1, d2, d3) in enumerate(ORDERS):
            row = opened(moved(moved(at, d2, 4 - back), d3, 2), d1)
            arrive(row, part, 23 + j)
            share(row, part, 14 + j)

    remote(low_total.at[theirs], low_total.at[theirs], rep, 5, pair).wait_recv()
    remote(layer_total.at[:, other], layer_total.at[:, other], rep, 6, pair).wait_recv()
    for copy in expected:
        copy.wait_recv()
    for copy in started + [to_pair, first, second, low_to_pair, low_to_twin, low_back, total_back]:
        copy.wait_send()
    loads[6].wait()


def finish_kernel(
    gathered, ge_v, me_v, low_total, layer_total, bt_v, gl_v, ml_v,
    mean_l, moment_l, weights_l, copy_l, mean_e, moment_e, weights_e,
    mean_lv, moment_lv, weights_lv, mean_v, moment_v, weights_v, sem, sem_e,
):
    rows = ge_v.shape[0]
    copies = []

    def put(src, dst, s):
        copy = pltpu.make_async_copy(src, dst, s)
        copy.start()
        copies.append(copy)

    put(gathered, copy_l, sem.at[0])
    basis = bt_v[...]
    high = basis.astype(jnp.bfloat16)
    none = jnp.zeros_like(high)
    left = jnp.concatenate([high, none, high, none], 0)
    right = jnp.concatenate([none, high, none, high], 0)
    for n, start in enumerate(range(0, rows, 128)):
        size = min(128, rows - start)
        packed = low_total[pl.ds(start % HALF, size), :] / 4
        top = packed.astype(jnp.bfloat16)
        rest = (packed - top.astype(jnp.float32)).astype(jnp.bfloat16)
        at = pl.ds(start, size)
        mean = jnp.dot(
            jnp.concatenate([top, rest], 1), left if start < HALF else right, preferred_element_type=jnp.float32
        )
        moment, weights = outer_update(mean, me_v[at, :], ge_v[at, :])
        for k, (value, buf, out) in enumerate(
            ((mean, mean_v, mean_e), (moment, moment_v, moment_e), (weights, weights_v, weights_e))
        ):
            buf[at, :] = value
            put(buf.at[at], out.at[at], sem_e.at[3 * n + k])
    mean = layer_total[...] / 4
    moment, weights = outer_update(mean, ml_v[...], gl_v[...])
    for k, (value, buf, out) in enumerate(
        ((mean, mean_lv, mean_l), (moment, moment_lv, moment_l), (weights, weights_lv, weights_l))
    ):
        buf[...] = value
        put(buf, out, sem.at[1 + k])
    for copy in copies:
        copy.wait()


def body(local_layers, global_layers, momentum_layers, local_embed, global_embed, momentum_embed, proj_basis):
    rows = global_embed.shape[0]
    grouped = (2, 2, 24, 768)
    ll, gl, ml = (a.reshape(grouped) for a in (local_layers, global_layers, momentum_layers))
    bt = proj_basis.T
    f32, bf16 = jnp.float32, jnp.bfloat16
    dma = pltpu.SemaphoreType.DMA
    kept = pl.pallas_call(
        exchange_kernel,
        out_shape=(
            pltpu.VMEM((2, 2, 2, 4, 4, 3, 8, 768), bf16),
            pltpu.VMEM((rows, 768), f32),
            pltpu.VMEM((rows, 768), f32),
            pltpu.VMEM((HALF, 128), f32),
            pltpu.VMEM(grouped, f32),
            pltpu.VMEM((64, 768), f32),
            pltpu.VMEM(grouped, f32),
            pltpu.VMEM(grouped, f32),
        ),
        in_specs=[HBM] * 7,
        out_specs=(VMEM,) * 8,
        scratch_shapes=[
            pltpu.VMEM((2, 24, 768), f32),
            pltpu.VMEM((2, 24, 768), f32),
            pltpu.VMEM((2, 24, 768), bf16),
            pltpu.VMEM((2, 24, 768), bf16),
            pltpu.VMEM((rows * 6, 128), f32),
            pltpu.VMEM((HALF, 128), f32),
            pltpu.VMEM((HALF // 2, 128), f32),
            pltpu.VMEM((HALF // 2, 128), bf16),
            pltpu.VMEM((HALF // 2, 128), bf16),
            dma((7,)),
            dma((7,)),
            dma((7,)),
            dma((81,)),
            dma((81,)),
            dma((57,)),
            dma((57,)),
        ],
        compiler_params=pltpu.CompilerParams(
            collective_id=0, has_side_effects=True, vmem_limit_bytes=52 << 20
        ),
        name="exchange",
    )(ll, gl, ml, local_embed.reshape(rows * 6, 128), global_embed, momentum_embed, bt)
    outs = pl.pallas_call(
        finish_kernel,
        out_shape=(
            *[jax.ShapeDtypeStruct(grouped, f32)] * 3,
            jax.ShapeDtypeStruct((2, 2, 2, 4, 4, 3, 8, 768), bf16),
            *[jax.ShapeDtypeStruct((rows, 768), f32)] * 3,
        ),
        in_specs=[VMEM] * 8,
        out_specs=(HBM,) * 7,
        scratch_shapes=[pltpu.VMEM(grouped, f32)] * 3 + [pltpu.VMEM((rows, 768), f32)] * 3 + [dma((4,)), dma((24,))],
        compiler_params=pltpu.CompilerParams(vmem_limit_bytes=24 << 20),
        name="finish",
    )(*kept)
    layers = [a.reshape(4, 24, 768) for a in outs[:3]]
    return (*layers, outs[3].reshape(4, 768, 768), *outs[4:])


def solution(mesh):
    in_specs = (
        P("rep", None, "shard", None),
        P(None, "shard", None),
        P(None, "shard", None),
        P("rep", "shard", None),
        P("shard", None),
        P("shard", None),
        P(),
    )
    out_specs = (
        P(None, "shard", None),
        P(None, "shard", None),
        P(None, "shard", None),
        P(),
        P("shard", None),
        P("shard", None),
        P("shard", None),
    )
    return jax.shard_map(body, mesh=mesh, in_specs=in_specs, out_specs=out_specs, check_vma=False)
```

```python
import functools

import jax
import jax.numpy as jnp
from jax import lax
from jax.experimental import pallas as pl
from jax.experimental.pallas import tpu as pltpu
from jax.sharding import PartitionSpec as P

OUTER_MOMENTUM = 0.9
OUTER_RATE = 0.7
MESH = pl.DeviceIdType.MESH
HBM = pl.BlockSpec(memory_space=pltpu.HBM)
VMEM = pl.BlockSpec(memory_space=pltpu.VMEM)
X, Y, Z = 0, 1, 2
ORDERS = ((X, Y, Z), (Y, Z, X), (Z, X, Y))
DELTAS = (1, 3, 2)
HALF = 512


def outer_update(mean_diff, momentum, weights):
    new_moment = OUTER_MOMENTUM * momentum + mean_diff
    new_weights = weights - OUTER_RATE * (mean_diff + OUTER_MOMENTUM * new_moment)
    return (new_moment, new_weights)


def where_am_i():
    rep, shard = lax.axis_index("rep"), lax.axis_index("shard")
    z_low, core = lax.div(rep, 2), lax.rem(rep, 2)
    z_high, x, y = lax.div(shard, 16), lax.rem(lax.div(shard, 4), 4), lax.rem(shard, 4)
    return [x, y, z_high * 2 + z_low], core


def device(at, core):
    x, y, z = at
    return (lax.rem(z, 2) * 2 + core, lax.div(z, 2) * 16 + x * 4 + y)


def moved(at, axis, step):
    return [lax.rem(c + step, 4) if i == axis else c for i, c in enumerate(at)]


def piece(gathered, at, core, part):
    x, y, z = (slice(None) if c is None else c for c in at)
    z_low, z_high = (z, z) if isinstance(z, slice) else (lax.rem(z, 2), lax.div(z, 2))
    return gathered.at[z_low, core, z_high, x, y, part]


def exchange_kernel(
    ll, gl, ml, le, ge, me, bt,
    gathered, ge_v, me_v, low_total, layer_total, bt_v, gl_v, ml_v,
    ll_v, ll_other, part_sum, part_other, le_v, low, low_in, low_half, low_other,
    load_sem, rep_send, rep_recv, ring_send, ring_recv, pair_send, pair_recv,
):
    at, core = where_am_i()
    other = 1 - core
    z_low = lax.rem(at[Z], 2)
    twin_at = [at[X], at[Y], at[Z] + 1 - 2 * z_low]
    pair, twin = device(at, other), device(twin_at, core)
    rows = ge.shape[0]

    def remote(src, dst, sems, i, to):
        send, recv = sems
        return pltpu.make_async_remote_copy(src, dst, send.at[i], recv.at[i], device_id=to, device_id_type=MESH)

    loads = [
        pltpu.make_async_copy(ll.at[:, core], ll_v, load_sem.at[0]),
        pltpu.make_async_copy(gl, gl_v, load_sem.at[1]),
        pltpu.make_async_copy(ml, ml_v, load_sem.at[2]),
        pltpu.make_async_copy(bt, bt_v, load_sem.at[3]),
        pltpu.make_async_copy(le, le_v, load_sem.at[4]),
        pltpu.make_async_copy(ge, ge_v, load_sem.at[5]),
        pltpu.make_async_copy(me, me_v, load_sem.at[6]),
    ]
    for load in loads[:6]:
        load.start()

    barrier = pltpu.get_barrier_semaphore()
    peers = [pair] + [device(moved(at, axis, step), core) for axis in (X, Y, Z) for step in DELTAS]
    for peer in peers:
        pl.semaphore_signal(barrier, inc=1, device_id=peer, device_id_type=MESH)
    pl.semaphore_wait(barrier, len(peers))

    rep = (rep_send, rep_recv)
    to_pair = remote(ll.at[:, other], ll_other, rep, 0, pair)
    to_pair.start()
    loads[0].wait()
    loads[1].wait()
    to_pair.wait_recv()
    weights = gl_v[:, core]
    part_sum[...] = ((weights - ll_v[...]) + (weights - ll_other[...])).astype(jnp.bfloat16)
    first = remote(part_sum.at[1 - z_low], part_other.at[1 - z_low], rep, 1, twin)
    second = remote(part_sum.at[z_low], part_other.at[z_low], rep, 2, twin)
    first.start()
    second.start()

    loads[3].wait()
    loads[4].wait()
    loads[5].wait()
    loads[6].start()
    basis = bt_v[...].astype(jnp.bfloat16)
    none = jnp.zeros_like(basis)
    left, right = jnp.concatenate([basis, none], 0), jnp.concatenate([none, basis], 0)
    nt = (((1,), (1,)), ((), ()))

    def local_rows(start, size):
        return jnp.concatenate([le_v[pl.ds(6 * start + c, size, 6), :] for c in range(6)], 1)

    for start in range(0, HALF, 128):
        tail = min(128, rows - HALF - start)
        a, b = pl.ds(start, 128), pl.ds(HALF + start, tail)
        da = (ge_v[a, :] - local_rows(start, 128)).astype(jnp.bfloat16)
        db = (ge_v[b, :] - local_rows(HALF + start, tail)).astype(jnp.bfloat16)
        pa = lax.dot_general(da, left, nt, preferred_element_type=jnp.float32)
        pb = lax.dot_general(db, right, nt, preferred_element_type=jnp.float32)
        low[a, :] = pa
        low[pl.ds(start, tail), :] = low[pl.ds(start, tail), :] + pb
    quarter = HALF // 2
    mine, theirs = pl.ds(core * quarter, quarter), pl.ds(other * quarter, quarter)
    low_to_pair = remote(low.at[theirs], low_in, rep, 3, pair)
    low_to_pair.start()

    loads[2].wait()
    first_in = remote(part_sum.at[z_low], part_other.at[z_low], rep, 1, twin)
    first_in.wait_recv()
    mean = (part_sum[z_low].astype(jnp.float32) + part_other[z_low].astype(jnp.float32)) / 4
    _, weights = outer_update(mean, ml_v[z_low, core], gl_v[z_low, core])
    gathered[z_low, core, lax.div(at[Z], 2), at[X], at[Y]] = weights.astype(jnp.bfloat16).reshape(3, 8, 768)

    ring, pairs = (ring_send, ring_recv), (pair_send, pair_recv)
    started, expected = [], []

    def send(where, part, slot, to):
        copy = remote(piece(gathered, where, core, part), piece(gathered, where, core, part), ring, part * 27 + slot, to)
        copy.start()
        started.append(copy)

    def arrive(where, part, slot):
        ref = piece(gathered, where, core, part)
        remote(ref, ref, ring, part * 27 + slot, pair).wait_recv()

    def share(where, part, slot):
        ref = piece(gathered, where, core, part)
        copy = remote(ref, ref, pairs, part * 19 + slot, pair)
        copy.start()
        started.append(copy)
        back = piece(gathered, where, other, part)
        expected.append(remote(back, back, pairs, part * 19 + slot, pair))

    def opened(where, *axes):
        return [None if i in axes else c for i, c in enumerate(where)]

    for part, (d1, d2, d3) in enumerate(ORDERS):
        for i, step in enumerate(DELTAS):
            send(at, part, i, device(moved(at, d1, step), core))
    for part in range(3):
        share(at, part, 18)

    low_to_pair.wait_recv()
    half = low[mine, :] + low_in[...]
    low_half[...] = half.astype(jnp.bfloat16)
    low_to_twin = remote(low_half, low_other, rep, 4, twin)
    low_to_twin.start()

    for part, (d1, d2, d3) in enumerate(ORDERS):
        chunks = [moved(at, d1, 4 - back) for back in DELTAS]
        for i, chunk in enumerate(chunks):
            arrive(chunk, part, i)
        row = opened(at, d1)
        for j, step in enumerate(DELTAS):
            send(row, part, 3 + j, device(moved(at, d2, step), core))
        for i, step in enumerate((1, 3)):
            send(row, part, 15 + i, device(moved(at, d3, step), core))
        for i, chunk in enumerate(chunks):
            share(chunk, part, i)

    for j, back in enumerate(DELTAS):
        for part, (d1, d2, d3) in enumerate(ORDERS):
            row = opened(moved(at, d2, 4 - back), d1)
            arrive(row, part, 3 + j)
            for i, step in enumerate((1, 3)):
                send(row, part, 17 + 2 * j + i, device(moved(at, d3, step), core))
            share(row, part, 3 + j)

    low_to_twin.wait_recv()
    low_total[mine, :] = low_half[...].astype(jnp.float32) + low_other[...].astype(jnp.float32)
    low_back = remote(low_total.at[mine], low_total.at[mine], rep, 5, pair)
    low_back.start()

    second_in = remote(part_sum.at[1 - z_low], part_other.at[1 - z_low], rep, 2, twin)
    second_in.wait_recv()
    layer_total[:, core] = part_sum[...].astype(jnp.float32) + part_other[...].astype(jnp.float32)
    total_back = remote(layer_total.at[:, core], layer_total.at[:, core], rep, 6, pair)
    total_back.start()

    for j, back in enumerate((0,) + DELTAS):
        for part, (d1, d2, d3) in enumerate(ORDERS):
            for i, step in enumerate((1, 3)):
                row = opened(moved(moved(at, d2, 4 - back), d3, 4 - step), d1)
                arrive(row, part, 15 + 2 * j + i)
                if j // 2 == i:
                    send(row, part, 23 + j, device(moved(at, d3, step), core))
                share(row, part, 6 + 2 * j + i)
    for j, back in enumerate((0,) + DELTAS):
        for part, (d1, d2, d3) in enumerate(ORDERS):
            row = opened(moved(moved(at, d2, 4 - back), d3, 2), d1)
            arrive(row, part, 23 + j)
            share(row, part, 14 + j)

    remote(low_total.at[theirs], low_total.at[theirs], rep, 5, pair).wait_recv()
    remote(layer_total.at[:, other], layer_total.at[:, other], rep, 6, pair).wait_recv()
    for copy in expected:
        copy.wait_recv()
    for copy in started + [to_pair, first, second, low_to_pair, low_to_twin, low_back, total_back]:
        copy.wait_send()
    loads[6].wait()


def finish_kernel(
    gathered, ge_v, me_v, low_total, layer_total, bt_v, gl_v, ml_v,
    mean_l, moment_l, weights_l, copy_l, mean_e, moment_e, weights_e,
    mean_lv, moment_lv, weights_lv, mean_v, moment_v, weights_v, sem, sem_e,
):
    rows = ge_v.shape[0]
    copies = []

    def put(src, dst, s):
        copy = pltpu.make_async_copy(src, dst, s)
        copy.start()
        copies.append(copy)

    put(gathered, copy_l, sem.at[0])
    basis = bt_v[...]
    high = basis.astype(jnp.bfloat16)
    none = jnp.zeros_like(high)
    left = jnp.concatenate([high, none, high, none], 0)
    right = jnp.concatenate([none, high, none, high], 0)
    for n, start in enumerate(range(0, rows, 128)):
        size = min(128, rows - start)
        packed = low_total[pl.ds(start % HALF, size), :] / 4
        top = packed.astype(jnp.bfloat16)
        rest = (packed - top.astype(jnp.float32)).astype(jnp.bfloat16)
        at = pl.ds(start, size)
        mean = jnp.dot(
            jnp.concatenate([top, rest], 1), left if start < HALF else right, preferred_element_type=jnp.float32
        )
        moment, weights = outer_update(mean, me_v[at, :], ge_v[at, :])
        for k, (value, buf, out) in enumerate(
            ((mean, mean_v, mean_e), (moment, moment_v, moment_e), (weights, weights_v, weights_e))
        ):
            buf[at, :] = value
            put(buf.at[at], out.at[at], sem_e.at[3 * n + k])
    mean = layer_total[...] / 4
    moment, weights = outer_update(mean, ml_v[...], gl_v[...])
    for k, (value, buf, out) in enumerate(
        ((mean, mean_lv, mean_l), (moment, moment_lv, moment_l), (weights, weights_lv, weights_l))
    ):
        buf[...] = value
        put(buf, out, sem.at[1 + k])
    for copy in copies:
        copy.wait()


def body(local_layers, global_layers, momentum_layers, local_embed, global_embed, momentum_embed, proj_basis):
    rows = global_embed.shape[0]
    grouped = (2, 2, 24, 768)
    ll, gl, ml = (a.reshape(grouped) for a in (local_layers, global_layers, momentum_layers))
    bt = proj_basis.T
    f32, bf16 = jnp.float32, jnp.bfloat16
    dma = pltpu.SemaphoreType.DMA
    kept = pl.pallas_call(
        exchange_kernel,
        out_shape=(
            pltpu.VMEM((2, 2, 2, 4, 4, 3, 8, 768), bf16),
            pltpu.VMEM((rows, 768), f32),
            pltpu.VMEM((rows, 768), f32),
            pltpu.VMEM((HALF, 128), f32),
            pltpu.VMEM(grouped, f32),
            pltpu.VMEM((64, 768), f32),
            pltpu.VMEM(grouped, f32),
            pltpu.VMEM(grouped, f32),
        ),
        in_specs=[HBM] * 7,
        out_specs=(VMEM,) * 8,
        scratch_shapes=[
            pltpu.VMEM((2, 24, 768), f32),
            pltpu.VMEM((2, 24, 768), f32),
            pltpu.VMEM((2, 24, 768), bf16),
            pltpu.VMEM((2, 24, 768), bf16),
            pltpu.VMEM((rows * 6, 128), f32),
            pltpu.VMEM((HALF, 128), f32),
            pltpu.VMEM((HALF // 2, 128), f32),
            pltpu.VMEM((HALF // 2, 128), bf16),
            pltpu.VMEM((HALF // 2, 128), bf16),
            dma((7,)),
            dma((7,)),
            dma((7,)),
            dma((81,)),
            dma((81,)),
            dma((57,)),
            dma((57,)),
        ],
        compiler_params=pltpu.CompilerParams(
            collective_id=0, has_side_effects=True, vmem_limit_bytes=52 << 20
        ),
        name="exchange",
    )(ll, gl, ml, local_embed.reshape(rows * 6, 128), global_embed, momentum_embed, bt)
    outs = pl.pallas_call(
        finish_kernel,
        out_shape=(
            *[jax.ShapeDtypeStruct(grouped, f32)] * 3,
            jax.ShapeDtypeStruct((2, 2, 2, 4, 4, 3, 8, 768), bf16),
            *[jax.ShapeDtypeStruct((rows, 768), f32)] * 3,
        ),
        in_specs=[VMEM] * 8,
        out_specs=(HBM,) * 7,
        scratch_shapes=[pltpu.VMEM(grouped, f32)] * 3 + [pltpu.VMEM((rows, 768), f32)] * 3 + [dma((4,)), dma((24,))],
        compiler_params=pltpu.CompilerParams(vmem_limit_bytes=24 << 20),
        name="finish",
    )(*kept)
    layers = [a.reshape(4, 24, 768) for a in outs[:3]]
    return (*layers, outs[3].reshape(4, 768, 768), *outs[4:])


def solution(mesh):
    in_specs = (
        P("rep", None, "shard", None),
        P(None, "shard", None),
        P(None, "shard", None),
        P("rep", "shard", None),
        P("shard", None),
        P("shard", None),
        P(),
    )
    out_specs = (
        P(None, "shard", None),
        P(None, "shard", None),
        P(None, "shard", None),
        P(),
        P("shard", None),
        P("shard", None),
        P("shard", None),
    )
    return jax.shard_map(body, mesh=mesh, in_specs=in_specs, out_specs=out_specs, check_vma=False)
```

```python
import functools

import jax
import jax.numpy as jnp
from jax import lax
from jax.experimental import pallas as pl
from jax.experimental.pallas import tpu as pltpu
from jax.sharding import PartitionSpec as P

OUTER_MOMENTUM = 0.9
OUTER_RATE = 0.7
MESH = pl.DeviceIdType.MESH
HBM = pl.BlockSpec(memory_space=pltpu.HBM)
VMEM = pl.BlockSpec(memory_space=pltpu.VMEM)
X, Y, Z = 0, 1, 2
ORDERS = ((X, Y, Z), (Y, Z, X), (Z, X, Y))
DELTAS = (1, 3, 2)
HALF = 512


def outer_update(mean_diff, momentum, weights):
    new_moment = OUTER_MOMENTUM * momentum + mean_diff
    new_weights = weights - OUTER_RATE * (mean_diff + OUTER_MOMENTUM * new_moment)
    return (new_moment, new_weights)


def where_am_i():
    rep, shard = lax.axis_index("rep"), lax.axis_index("shard")
    z_low, core = lax.div(rep, 2), lax.rem(rep, 2)
    z_high, x, y = lax.div(shard, 16), lax.rem(lax.div(shard, 4), 4), lax.rem(shard, 4)
    return [x, y, z_high * 2 + z_low], core


def device(at, core):
    x, y, z = at
    return (lax.rem(z, 2) * 2 + core, lax.div(z, 2) * 16 + x * 4 + y)


def moved(at, axis, step):
    return [lax.rem(c + step, 4) if i == axis else c for i, c in enumerate(at)]


def piece(gathered, at, core, part):
    x, y, z = (slice(None) if c is None else c for c in at)
    z_low, z_high = (z, z) if isinstance(z, slice) else (lax.rem(z, 2), lax.div(z, 2))
    return gathered.at[z_low, core, z_high, x, y, part]


def exchange_kernel(
    ll, gl, ml, le, ge, me, bt,
    gathered, ge_v, me_v, low_total, layer_total, bt_v, gl_v, ml_v,
    ll_v, ll_other, part_sum, part_other, le_v, low, low_in, low_half, low_other,
    load_sem, rep_send, rep_recv, ring_send, ring_recv, pair_send, pair_recv,
):
    at, core = where_am_i()
    other = 1 - core
    z_low = lax.rem(at[Z], 2)
    twin_at = [at[X], at[Y], at[Z] + 1 - 2 * z_low]
    pair, twin = device(at, other), device(twin_at, core)
    rows = ge.shape[0]

    def remote(src, dst, sems, i, to):
        send, recv = sems
        return pltpu.make_async_remote_copy(src, dst, send.at[i], recv.at[i], device_id=to, device_id_type=MESH)

    loads = [
        pltpu.make_async_copy(ll.at[:, core], ll_v, load_sem.at[0]),
        pltpu.make_async_copy(gl, gl_v, load_sem.at[1]),
        pltpu.make_async_copy(ml, ml_v, load_sem.at[2]),
        pltpu.make_async_copy(bt, bt_v, load_sem.at[3]),
        pltpu.make_async_copy(le, le_v, load_sem.at[4]),
        pltpu.make_async_copy(ge, ge_v, load_sem.at[5]),
        pltpu.make_async_copy(me, me_v, load_sem.at[6]),
    ]
    for load in loads[:6]:
        load.start()

    barrier = pltpu.get_barrier_semaphore()
    peers = [pair] + [device(moved(at, axis, step), core) for axis in (X, Y, Z) for step in DELTAS]
    for peer in peers:
        pl.semaphore_signal(barrier, inc=1, device_id=peer, device_id_type=MESH)
    pl.semaphore_wait(barrier, len(peers))

    rep = (rep_send, rep_recv)
    to_pair = remote(ll.at[:, other], ll_other, rep, 0, pair)
    to_pair.start()
    loads[0].wait()
    loads[1].wait()
    to_pair.wait_recv()
    weights = gl_v[:, core]
    part_sum[...] = ((weights - ll_v[...]) + (weights - ll_other[...])).astype(jnp.bfloat16)
    first = remote(part_sum.at[1 - z_low], part_other.at[1 - z_low], rep, 1, twin)
    second = remote(part_sum.at[z_low], part_other.at[z_low], rep, 2, twin)
    first.start()
    second.start()

    loads[2].wait()
    first_in = remote(part_sum.at[z_low], part_other.at[z_low], rep, 1, twin)
    first_in.wait_recv()
    mean = (part_sum[z_low].astype(jnp.float32) + part_other[z_low].astype(jnp.float32)) / 4
    _, weights = outer_update(mean, ml_v[z_low, core], gl_v[z_low, core])
    gathered[z_low, core, lax.div(at[Z], 2), at[X], at[Y]] = weights.astype(jnp.bfloat16).reshape(3, 8, 768)

    ring, pairs = (ring_send, ring_recv), (pair_send, pair_recv)
    started, expected = [], []

    def send(where, part, slot, to):
        copy = remote(piece(gathered, where, core, part), piece(gathered, where, core, part), ring, part * 27 + slot, to)
        copy.start()
        started.append(copy)

    def arrive(where, part, slot):
        ref = piece(gathered, where, core, part)
        remote(ref, ref, ring, part * 27 + slot, pair).wait_recv()

    def share(where, part, slot):
        ref = piece(gathered, where, core, part)
        copy = remote(ref, ref, pairs, part * 19 + slot, pair)
        copy.start()
        started.append(copy)
        back = piece(gathered, where, other, part)
        expected.append(remote(back, back, pairs, part * 19 + slot, pair))

    def opened(where, *axes):
        return [None if i in axes else c for i, c in enumerate(where)]

    for part, (d1, d2, d3) in enumerate(ORDERS):
        for i, step in enumerate(DELTAS):
            send(at, part, i, device(moved(at, d1, step), core))
    for part, (d1, d2, d3) in enumerate(ORDERS):
        for j, step in enumerate(DELTAS):
            send(at, part, 3 + 4 * j, device(moved(at, d2, step), core))
    for part in range(3):
        share(at, part, 18)

    loads[3].wait()
    loads[4].wait()
    loads[5].wait()
    loads[6].start()
    basis = bt_v[...].astype(jnp.bfloat16)
    none = jnp.zeros_like(basis)
    left, right = jnp.concatenate([basis, none], 0), jnp.concatenate([none, basis], 0)
    nt = (((1,), (1,)), ((), ()))

    def local_rows(start, size):
        return jnp.concatenate([le_v[pl.ds(6 * start + c, size, 6), :] for c in range(6)], 1)

    for start in range(0, HALF, 128):
        tail = min(128, rows - HALF - start)
        a, b = pl.ds(start, 128), pl.ds(HALF + start, tail)
        da = (ge_v[a, :] - local_rows(start, 128)).astype(jnp.bfloat16)
        db = (ge_v[b, :] - local_rows(HALF + start, tail)).astype(jnp.bfloat16)
        pa = lax.dot_general(da, left, nt, preferred_element_type=jnp.float32)
        pb = lax.dot_general(db, right, nt, preferred_element_type=jnp.float32)
        low[a, :] = pa
        low[pl.ds(start, tail), :] = low[pl.ds(start, tail), :] + pb
    quarter = HALF // 2
    mine, theirs = pl.ds(core * quarter, quarter), pl.ds(other * quarter, quarter)
    low_to_pair = remote(low.at[theirs], low_in, rep, 3, pair)
    low_to_pair.start()

    for i, back in enumerate(DELTAS):
        for part, (d1, d2, d3) in enumerate(ORDERS):
            chunk = moved(at, d1, 4 - back)
            arrive(chunk, part, i)
            for j, step in enumerate(DELTAS):
                send(chunk, part, 4 + 4 * j + i, device(moved(at, d2, step), core))
            share(chunk, part, i)
    for part, (d1, d2, d3) in enumerate(ORDERS):
        for i, step in enumerate((1, 3)):
            send(opened(at, d1), part, 15 + i, device(moved(at, d3, step), core))

    low_to_pair.wait_recv()
    half = low[mine, :] + low_in[...]
    low_half[...] = half.astype(jnp.bfloat16)
    low_to_twin = remote(low_half, low_other, rep, 4, twin)
    low_to_twin.start()

    for j, back in enumerate(DELTAS):
        for part, (d1, d2, d3) in enumerate(ORDERS):
            first_chunk = moved(at, d2, 4 - back)
            for k, across in enumerate((0,) + DELTAS):
                arrive(moved(first_chunk, d1, 4 - across), part, 3 + 4 * j + k)
            row = opened(first_chunk, d1)
            for i, step in enumerate((1, 3)):
                send(row, part, 17 + 2 * j + i, device(moved(at, d3, step), core))
            share(row, part, 3 + j)

    low_to_twin.wait_recv()
    low_total[mine, :] = low_half[...].astype(jnp.float32) + low_other[...].astype(jnp.float32)
    low_back = remote(low_total.at[mine], low_total.at[mine], rep, 5, pair)
    low_back.start()

    second_in = remote(part_sum.at[1 - z_low], part_other.at[1 - z_low], rep, 2, twin)
    second_in.wait_recv()
    layer_total[:, core] = part_sum[...].astype(jnp.float32) + part_other[...].astype(jnp.float32)
    total_back = remote(layer_total.at[:, core], layer_total.at[:, core], rep, 6, pair)
    total_back.start()

    for j, back in enumerate((0,) + DELTAS):
        for part, (d1, d2, d3) in enumerate(ORDERS):
            for i, step in enumerate((1, 3)):
                row = opened(moved(moved(at, d2, 4 - back), d3, 4 - step), d1)
                arrive(row, part, 15 + 2 * j + i)
                if j // 2 == i:
                    send(row, part, 23 + j, device(moved(at, d3, step), core))
                share(row, part, 6 + 2 * j + i)
    for j, back in enumerate((0,) + DELTAS):
        for part, (d1, d2, d3) in enumerate(ORDERS):
            row = opened(moved(moved(at, d2, 4 - back), d3, 2), d1)
            arrive(row, part, 23 + j)
            share(row, part, 14 + j)

    remote(low_total.at[theirs], low_total.at[theirs], rep, 5, pair).wait_recv()
    remote(layer_total.at[:, other], layer_total.at[:, other], rep, 6, pair).wait_recv()
    for copy in expected:
        copy.wait_recv()
    for copy in started + [to_pair, first, second, low_to_pair, low_to_twin, low_back, total_back]:
        copy.wait_send()
    loads[6].wait()


def finish_kernel(
    gathered, ge_v, me_v, low_total, layer_total, bt_v, gl_v, ml_v,
    mean_l, moment_l, weights_l, copy_l, mean_e, moment_e, weights_e,
    mean_lv, moment_lv, weights_lv, mean_v, moment_v, weights_v, sem, sem_e,
):
    rows = ge_v.shape[0]
    copies = []

    def put(src, dst, s):
        copy = pltpu.make_async_copy(src, dst, s)
        copy.start()
        copies.append(copy)

    put(gathered, copy_l, sem.at[0])
    basis = bt_v[...]
    high = basis.astype(jnp.bfloat16)
    none = jnp.zeros_like(high)
    left = jnp.concatenate([high, none, high, none], 0)
    right = jnp.concatenate([none, high, none, high], 0)
    for n, start in enumerate(range(0, rows, 128)):
        size = min(128, rows - start)
        packed = low_total[pl.ds(start % HALF, size), :] / 4
        top = packed.astype(jnp.bfloat16)
        rest = (packed - top.astype(jnp.float32)).astype(jnp.bfloat16)
        at = pl.ds(start, size)
        mean = jnp.dot(
            jnp.concatenate([top, rest], 1), left if start < HALF else right, preferred_element_type=jnp.float32
        )
        moment, weights = outer_update(mean, me_v[at, :], ge_v[at, :])
        for k, (value, buf, out) in enumerate(
            ((mean, mean_v, mean_e), (moment, moment_v, moment_e), (weights, weights_v, weights_e))
        ):
            buf[at, :] = value
            put(buf.at[at], out.at[at], sem_e.at[3 * n + k])
    mean = layer_total[...] / 4
    moment, weights = outer_update(mean, ml_v[...], gl_v[...])
    for k, (value, buf, out) in enumerate(
        ((mean, mean_lv, mean_l), (moment, moment_lv, moment_l), (weights, weights_lv, weights_l))
    ):
        buf[...] = value
        put(buf, out, sem.at[1 + k])
    for copy in copies:
        copy.wait()


def body(local_layers, global_layers, momentum_layers, local_embed, global_embed, momentum_embed, proj_basis):
    rows = global_embed.shape[0]
    grouped = (2, 2, 24, 768)
    ll, gl, ml = (a.reshape(grouped) for a in (local_layers, global_layers, momentum_layers))
    bt = proj_basis.T
    f32, bf16 = jnp.float32, jnp.bfloat16
    dma = pltpu.SemaphoreType.DMA
    kept = pl.pallas_call(
        exchange_kernel,
        out_shape=(
            pltpu.VMEM((2, 2, 2, 4, 4, 3, 8, 768), bf16),
            pltpu.VMEM((rows, 768), f32),
            pltpu.VMEM((rows, 768), f32),
            pltpu.VMEM((HALF, 128), f32),
            pltpu.VMEM(grouped, f32),
            pltpu.VMEM((64, 768), f32),
            pltpu.VMEM(grouped, f32),
            pltpu.VMEM(grouped, f32),
        ),
        in_specs=[HBM] * 7,
        out_specs=(VMEM,) * 8,
        scratch_shapes=[
            pltpu.VMEM((2, 24, 768), f32),
            pltpu.VMEM((2, 24, 768), f32),
            pltpu.VMEM((2, 24, 768), bf16),
            pltpu.VMEM((2, 24, 768), bf16),
            pltpu.VMEM((rows * 6, 128), f32),
            pltpu.VMEM((HALF, 128), f32),
            pltpu.VMEM((HALF // 2, 128), f32),
            pltpu.VMEM((HALF // 2, 128), bf16),
            pltpu.VMEM((HALF // 2, 128), bf16),
            dma((7,)),
            dma((7,)),
            dma((7,)),
            dma((81,)),
            dma((81,)),
            dma((57,)),
            dma((57,)),
        ],
        compiler_params=pltpu.CompilerParams(
            collective_id=0, has_side_effects=True, vmem_limit_bytes=52 << 20
        ),
        name="exchange",
    )(ll, gl, ml, local_embed.reshape(rows * 6, 128), global_embed, momentum_embed, bt)
    outs = pl.pallas_call(
        finish_kernel,
        out_shape=(
            *[jax.ShapeDtypeStruct(grouped, f32)] * 3,
            jax.ShapeDtypeStruct((2, 2, 2, 4, 4, 3, 8, 768), bf16),
            *[jax.ShapeDtypeStruct((rows, 768), f32)] * 3,
        ),
        in_specs=[VMEM] * 8,
        out_specs=(HBM,) * 7,
        scratch_shapes=[pltpu.VMEM(grouped, f32)] * 3 + [pltpu.VMEM((rows, 768), f32)] * 3 + [dma((4,)), dma((24,))],
        compiler_params=pltpu.CompilerParams(vmem_limit_bytes=24 << 20),
        name="finish",
    )(*kept)
    layers = [a.reshape(4, 24, 768) for a in outs[:3]]
    return (*layers, outs[3].reshape(4, 768, 768), *outs[4:])


def solution(mesh):
    in_specs = (
        P("rep", None, "shard", None),
        P(None, "shard", None),
        P(None, "shard", None),
        P("rep", "shard", None),
        P("shard", None),
        P("shard", None),
        P(),
    )
    out_specs = (
        P(None, "shard", None),
        P(None, "shard", None),
        P(None, "shard", None),
        P(),
        P("shard", None),
        P("shard", None),
        P("shard", None),
    )
    return jax.shard_map(body, mesh=mesh, in_specs=in_specs, out_specs=out_specs, check_vma=False)
```
